256 devices in a mesh: dp: 4 (over x), context: 16 (over y_lo, z), tensor: 4 (over y_hi, core).
Axes of the slice: x: 4, y: 4 (y_hi: 2, y_lo: 2; y = y_hi * 2 + y_lo), z: 8, core: 2. Of those that a mesh axis runs over, the one named last changes fastest.
Arguments:
- grad_out: bfloat16 [32768, 8192], P(('dp', 'context', 'tensor')), may hold values from -24 to 24
- queries: bfloat16 [32768, 1024], P(('dp', 'context'), 'tensor'), may hold values from -6 to 6
- attended: bfloat16 [32768, 1024], P(('dp', 'context'), 'tensor'), may hold values from -6 to 6
- keys: bfloat16 [32768, 128], P(('dp', 'context')), may hold values from -6 to 6
- values: bfloat16 [32768, 128], P(('dp', 'context')), may hold values from -6 to 6
- log_sums: float32 [8, 32768], P('tensor', ('dp', 'context')), may hold values from 1 to 3
- segment_ids: int32 [4, 8192], P('dp'), may hold values from 0 to 7, as said below
- w_out: bfloat16 [8192, 1024], P(('dp', 'context'), 'tensor'), may hold values from -0.0625 to 0.0625
- w_query: bfloat16 [1024, 8192], P('tensor', ('dp', 'context')), may hold values from -0.1875 to 0.1875
- w_key: bfloat16 [128, 8192], replicated, may hold values from -0.5 to 0.5
- w_value: bfloat16 [128, 8192], replicated, may hold values from -0.5 to 0.5
Outputs:
- grad_input: bfloat16 [32768, 8192], P(('dp', 'context', 'tensor'))
- out_proj_grad: float32 [8192, 1024], P(('dp', 'context'), 'tensor')
The draws below stay inside these ranges and needn't reach their ends.
Inputs may be any that keep to these rules, and one draw needn't show every extreme that they name: `segment_ids`: along the positions of a sequence the document number never falls; every sequence holds exactly 8 documents, numbered from 0.
All inputs are finite; a program needn't handle non-finite values.
Results may differ from the reference program's by a relative error of at most 0.02.
Values may be sent and summed in bfloat16 or wider, within the bound.
A program may use at most 128 MiB of HBM per device.

```python
import math
import jax
import jax.numpy as jnp
from jax import lax

D = 8192
HQ = 8
HEAD = 128
DOCS = 8
SPAN = 256
LENGTH = 8192
SEQS = 4
TOKENS = 32768
N_CONTEXT = 16
N_TENSOR = 4


def draw_segment_ids(key, part):
    seq_keys = jax.random.split(jax.random.fold_in(key, 17), SEQS)

    def one_sequence(seq_key):
        cuts = jax.random.permutation(seq_key, LENGTH - 1)[:DOCS - 1] + 1
        positions = jnp.arange(LENGTH, dtype=jnp.int32)
        return jnp.sum((positions[:, None] >= cuts[None, :]).astype(jnp.int32), axis=1).astype(jnp.int32)
    return jax.vmap(one_sequence)(seq_keys)


def raised(array, stream_key, source, target, parts, factor):
    def block_of(axis_at):
        return (jnp.arange(array.shape[axis_at]) // (array.shape[axis_at] // parts)).reshape((-1,) + (1,) * (array.ndim - 1 - axis_at))

    near = jax.random.permutation(stream_key, parts)[block_of(target)]
    second = (block_of(target) + parts // 2) % parts
    return jnp.where((block_of(source) == near) | (block_of(source) == second), factor * array, array)


def level_of(own_key, extent, cuts, least, largest):
    level, own = 1.0, jax.random.fold_in(own_key, 6)
    for position, parts in cuts:
        steps = jnp.exp(jax.random.uniform(jax.random.fold_in(own, position), (parts,), jnp.float32, least / len(cuts), largest / len(cuts)))
        level = level * jnp.repeat(steps, extent[position] // parts).reshape([-1 if axis == position else 1 for axis in range(len(extent))])
    return level


def centred(key, dims, scale, reach, cuts=(), held_as=jnp.bfloat16):
    values = scale * jax.random.normal(key, dims, jnp.float32)
    if cuts:
        values = values * level_of(key, dims, cuts, -0.22, 0.18)
    return jnp.clip(values, -reach, reach).astype(held_as)


def gaussian_with(stream_key, dims, scale, reach, shards, heavy, kind=jnp.bfloat16):
    entries = scale * jax.random.normal(stream_key, dims, jnp.float32)
    if shards:
        entries = entries * level_of(stream_key, dims, shards, -0.22, 0.18)
    return jnp.clip(raised(entries, jax.random.fold_in(stream_key, 3), *heavy), -reach, reach).astype(kind)


def setup_inputs(seed: int = 0) -> dict:
    arg_keys = jax.random.split(jax.random.key(seed), 12)
    return {
        "grad_out": gaussian_with(arg_keys[0], (TOKENS, D), 1.0, 24.0, ((0, 256),), (0, 1, 256, 6.0)),
        "queries": centred(arg_keys[1], (TOKENS, HQ * HEAD), 1.0, 6.0, ((0, 64), (1, 4))),
        "attended": centred(arg_keys[2], (TOKENS, HQ * HEAD), 1.0, 6.0, ((0, 64), (1, 4))),
        "keys": centred(arg_keys[3], (TOKENS, HEAD), 1.0, 6.0, ((0, 64),)),
        "values": centred(arg_keys[4], (TOKENS, HEAD), 1.0, 6.0, ((0, 64),)),
        "log_sums": jnp.clip(1.0 + 2.0 * jax.random.uniform(arg_keys[5], (HQ, TOKENS), jnp.float32) ** level_of(arg_keys[5], (HQ, TOKENS), ((0, 4), (1, 64)), -0.2, 0.2), 1.0, 3.0),
        "segment_ids": draw_segment_ids(jax.random.fold_in(arg_keys[11], 71), 0),
        "w_out": centred(arg_keys[7], (D, HQ * HEAD), D ** -0.5, 0.0625, ((0, 64), (1, 4))),
        "w_query": centred(arg_keys[8], (HQ * HEAD, D), (HQ * HEAD) ** -0.5, 0.1875, ((0, 4), (1, 64))),
        "w_key": centred(arg_keys[9], (HEAD, D), HEAD ** -0.5, 0.5),
        "w_value": centred(arg_keys[10], (HEAD, D), HEAD ** -0.5, 0.5),
    }


def to_natural(stored):
    width = stored.shape[1]
    blocks = stored.reshape(N_CONTEXT, 2, SPAN, width)
    return jnp.concatenate([blocks[:, 0], blocks[::-1, 1]], axis=0).reshape(LENGTH, width)

def to_stored(natural):
    width = natural.shape[1]
    blocks = natural.reshape(2 * N_CONTEXT, SPAN, width)
    return jnp.stack([blocks[:N_CONTEXT], blocks[N_CONTEXT:][::-1]], axis=1).reshape(LENGTH, width)

def sequence_grads(query_nat, dout_nat, lse_nat, delta_nat, key_nat, value_nat, seg_nat):
    inv_root = 1.0 / math.sqrt(HEAD)
    pad_keys = jnp.concatenate([jnp.zeros((SPAN, HEAD), key_nat.dtype), key_nat], axis=0)
    pad_values = jnp.concatenate([jnp.zeros((SPAN, HEAD), value_nat.dtype), value_nat], axis=0)
    pad_seg = jnp.concatenate([jnp.full((SPAN,), -1, jnp.int32), seg_nat.astype(jnp.int32)], axis=0)
    offsets = jnp.arange(SPAN, dtype=jnp.int32)
    key_offsets = jnp.arange(2 * SPAN, dtype=jnp.int32)

    def span_step(carry_acc, span_idx):
        key_acc, value_acc = carry_acc
        qstart = (span_idx * SPAN).astype(jnp.int32)
        query_blk = lax.dynamic_slice_in_dim(query_nat, qstart, SPAN, 0).astype(jnp.float32)
        dout_blk = lax.dynamic_slice_in_dim(dout_nat, qstart, SPAN, 0).astype(jnp.float32)
        lse_blk = lax.dynamic_slice_in_dim(lse_nat, qstart, SPAN, 1)
        delta_blk = lax.dynamic_slice_in_dim(delta_nat, qstart, SPAN, 1)
        key_blk = lax.dynamic_slice_in_dim(pad_keys, qstart, 2 * SPAN, 0).astype(jnp.float32)
        value_blk = lax.dynamic_slice_in_dim(pad_values, qstart, 2 * SPAN, 0).astype(jnp.float32)
        query_pos = qstart + offsets
        key_pos = qstart - SPAN + key_offsets
        seg_query = lax.dynamic_slice_in_dim(seg_nat.astype(jnp.int32), qstart, SPAN, 0)
        seg_key = lax.dynamic_slice_in_dim(pad_seg, qstart, 2 * SPAN, 0)
        allowed = (key_pos[None, :] <= query_pos[:, None]) & (key_pos[None, :] >= 0) & (seg_key[None, :] == seg_query[:, None])
        scores = jnp.einsum('qhe,ke->hqk', query_blk, key_blk) * inv_root
        prob_full = jnp.where(allowed[None], jnp.exp(scores - lse_blk[:, :, None]), 0.0)
        prob_low = lax.optimization_barrier(prob_full.astype(jnp.bfloat16)).astype(jnp.float32)
        dprobs = jnp.einsum('qhe,ke->hqk', dout_blk, value_blk)
        dscores = (prob_full * (dprobs - delta_blk[:, :, None])).astype(jnp.bfloat16)
        dscores = lax.optimization_barrier(dscores).astype(jnp.float32)
        dquery = (jnp.einsum('hqk,ke->qhe', dscores, key_blk) * inv_root).astype(jnp.bfloat16)
        key_heads = jnp.einsum('hqk,qhe->hke', dscores, query_blk) * inv_root
        value_heads = jnp.einsum('hqk,qhe->hke', prob_low, dout_blk)
        key_groups = key_heads.reshape(N_TENSOR, HQ // N_TENSOR, 2 * SPAN, HEAD).sum(axis=1)
        value_groups = value_heads.reshape(N_TENSOR, HQ // N_TENSOR, 2 * SPAN, HEAD).sum(axis=1)
        old_keys = lax.dynamic_slice_in_dim(key_acc, qstart, 2 * SPAN, 1)
        old_values = lax.dynamic_slice_in_dim(value_acc, qstart, 2 * SPAN, 1)
        key_acc = lax.dynamic_update_slice_in_dim(key_acc, old_keys + key_groups, qstart, 1)
        value_acc = lax.dynamic_update_slice_in_dim(value_acc, old_values + value_groups, qstart, 1)
        return ((key_acc, value_acc), dquery)
    zero_acc = jnp.zeros((N_TENSOR, LENGTH + SPAN, HEAD), jnp.float32)
    (key_acc, value_acc), dquery_blocks = lax.scan(span_step, (zero_acc, zero_acc), jnp.arange(2 * N_CONTEXT, dtype=jnp.int32))
    return (dquery_blocks.reshape(LENGTH, HQ * HEAD), key_acc[:, SPAN:], value_acc[:, SPAN:])

def reference(grad_out, queries, attended, keys, values, log_sums, segment_ids, w_out, w_query, w_key, w_value):
    group_cols = HQ // N_TENSOR * HEAD
    attn_grads = jnp.dot(grad_out, w_out, preferred_element_type=jnp.float32).astype(jnp.bfloat16)
    out_proj_grad = lax.dot_general(grad_out, attended, (((0,), (0,)), ((), ())), preferred_element_type=jnp.float32)
    row_delta = (attn_grads.astype(jnp.float32) * attended.astype(jnp.float32)).reshape(TOKENS, HQ, HEAD).sum(axis=2)
    results = []
    for seq_idx in range(SEQS):
        lower = seq_idx * LENGTH
        upper = lower + LENGTH
        query_nat = to_natural(queries[lower:upper]).reshape(LENGTH, HQ, HEAD)
        dout_nat = to_natural(attn_grads[lower:upper]).reshape(LENGTH, HQ, HEAD)
        lse_nat = to_natural(log_sums[:, lower:upper].T).T
        delta_nat = to_natural(row_delta[lower:upper]).T
        key_nat = to_natural(keys[lower:upper])
        value_nat = to_natural(values[lower:upper])
        dquery_nat, dkey_nat, dvalue_nat = sequence_grads(query_nat, dout_nat, lse_nat, delta_nat, key_nat, value_nat, segment_ids[seq_idx])
        dquery = to_stored(dquery_nat)
        summed = jnp.zeros((LENGTH, D), jnp.float32)
        for group in range(N_TENSOR):
            key_part = to_stored(dkey_nat[group].astype(jnp.bfloat16))
            value_part = to_stored(dvalue_nat[group].astype(jnp.bfloat16))
            cols = dquery[:, group * group_cols:(group + 1) * group_cols]
            part = jnp.dot(cols, w_query[group * group_cols:(group + 1) * group_cols], preferred_element_type=jnp.float32)
            part = part + jnp.dot(key_part, w_key, preferred_element_type=jnp.float32)
            part = part + jnp.dot(value_part, w_value, preferred_element_type=jnp.float32)
            summed = summed + lax.optimization_barrier(part.astype(jnp.bfloat16)).astype(jnp.float32)
        results.append(summed.astype(jnp.bfloat16))
    grad_input = jnp.concatenate(results, axis=0)
    return (grad_input, out_proj_grad)
```

```python
import functools
import math

import jax
import jax.numpy as jnp
from jax import lax
from jax.experimental import pallas as pl
from jax.experimental.pallas import tpu as pltpu
from jax.sharding import PartitionSpec as P

MESH = pl.DeviceIdType.MESH
BF = jnp.bfloat16
F32 = jnp.float32
NX, NY, NZ = 4, 4, 8
SPAN = 256
HD = 128
N_REMOTE = 200
N_LOCAL = 8


def wrap(i, n):
    return lax.rem(i + n, n)


class Links:
    def __init__(self, send, recv):
        self.send, self.recv, self.started = send, recv, []

    def copy(self, src, dst, dev):
        n = len(self.started)
        c = pltpu.make_async_remote_copy(
            src_ref=src,
            dst_ref=dst,
            send_sem=self.send.at[n],
            recv_sem=self.recv.at[n],
            device_id=dev,
            device_id_type=MESH,
        )
        c.start()
        self.started.append(c)
        return c


def ring_gather(links, n, i, slab, half, up, down, arrived=None):
    k = n // 2
    cp = links.copy(slab(i), slab(i), up)
    cm = links.copy(slab(i), slab(i), down)
    if arrived is not None:
        arrived(slab(i))
    yield
    for s in range(1, k):
        before, after = wrap(i - s, n), wrap(i + s, n)
        cp.wait_recv()
        got = slab(before)
        piece = got if s < k - 1 else got.at[0:half]
        cp = links.copy(piece, piece, up)
        if arrived is not None:
            arrived(got)
        cm.wait_recv()
        got = slab(after)
        piece = got if s < k - 1 else got.at[half : 2 * half]
        cm = links.copy(piece, piece, down)
        if arrived is not None:
            arrived(got)
        yield
    cp.wait_recv()
    cm.wait_recv()
    if arrived is not None:
        arrived(slab(wrap(i + k, n)))


def ring_reduce(links, n, i, slab, buf, half, up, down):
    k = n // 2
    far = wrap(i + k, n)
    cp = links.copy(slab(far).at[0:half], buf.at[0, 0, 0:half], up)
    cm = links.copy(slab(far).at[half : 2 * half], buf.at[1, 0, half : 2 * half], down)
    yield

    def add(dst, part):
        dst[...] = (dst[...].astype(F32) + part[...].astype(F32)).astype(BF)

    for step in range(1, k):
        s = k - step
        dst = slab(wrap(i + s, n))
        cp.wait_recv()
        if step == 1:
            add(dst.at[0:half], buf.at[0, 0, 0:half])
        else:
            add(dst, buf.at[0, step - 1])
        cp = links.copy(dst, buf.at[0, step], up)
        dst = slab(wrap(i - s, n))
        cm.wait_recv()
        if step == 1:
            add(dst.at[half : 2 * half], buf.at[1, 0, half : 2 * half])
        else:
            add(dst, buf.at[1, step - 1])
        cm = links.copy(dst, buf.at[1, step], down)
        yield
    cp.wait_recv()
    cm.wait_recv()
    dst = slab(i)
    dst[...] = (
        dst[...].astype(F32) + buf[0, k - 1].astype(F32) + buf[1, k - 1].astype(F32)
    ).astype(BF)


def contract(a, b, da, db):
    return lax.dot_general(a, b, (((da,), (db,)), ((), ())), preferred_element_type=F32)


def kernel(
    grad_out, queries, attended, keys, values, log_sums, seg, w_out, w_query, w_key, w_value,
    gin, dwo,
    tg, fwd, wv, qv, kvw, pb, raz, rax, ray, rbx, rbz, rby,
    halo, ag, att_t, acc, qkv, kvg, kvback, kvland, ab, send, recv, loc,
):
    x = lax.axis_index("dp")
    r = lax.axis_index("context")
    t = lax.axis_index("tensor")
    yl, z = lax.div(r, NZ), lax.rem(r, NZ)
    yh, core = lax.div(t, 2), lax.rem(t, 2)
    y = 2 * yh + yl
    other = 1 - core
    partner = 2 * (1 - yh) + core

    def dev(x, y, z, core):
        return {
            "dp": x,
            "context": lax.rem(y, 2) * NZ + z,
            "tensor": lax.div(y, 2) * 2 + core,
        }

    xp, xm = dev(wrap(x + 1, NX), y, z, core), dev(wrap(x - 1, NX), y, z, core)
    yp, ym = dev(x, wrap(y + 1, NY), z, core), dev(x, wrap(y - 1, NY), z, core)
    zp, zm = dev(x, y, wrap(z + 1, NZ), core), dev(x, y, wrap(z - 1, NZ), core)
    pair = dev(x, 2 * yh + 1 - yl, z, core)
    sib = dev(x, y, z, other)
    far = dev(x, wrap(y + 2, NY), z, core)
    far_sib = dev(x, wrap(y + 2, NY), z, other)
    n_ctx = 2 * NZ
    rp = {"dp": x, "context": wrap(r + 1, n_ctx), "tensor": t}
    rm = {"dp": x, "context": wrap(r - 1, n_ctx), "tensor": t}
    links = Links(send, recv)

    local = [
        pltpu.make_async_copy(w_out, wv.at[x, yl, z], loc.at[0]),
        pltpu.make_async_copy(w_query, qv.at[core, x, y, z], loc.at[1]),
        pltpu.make_async_copy(grad_out, tg.at[t], loc.at[2]),
        pltpu.make_async_copy(w_key, kvw.at[0:HD], loc.at[3]),
        pltpu.make_async_copy(w_value, kvw.at[HD : 2 * HD], loc.at[4]),
    ]
    for c in local:
        c.start()
    partners = (xp, xm, yp, ym, zp, zm, rp, rm, sib, far, far_sib)
    barrier = pltpu.get_barrier_semaphore()
    for d in partners:
        pl.semaphore_signal(barrier, inc=1, device_id=d, device_id_type=MESH)
    att_t[...] = attended[...].astype(F32).T.astype(BF)
    pl.semaphore_wait(barrier, len(partners))

    rows = 16
    n_pieces = 64 // rows
    sib_waits = []

    def grads_stream():
        first = []
        for k in range(n_pieces):
            a, b = pl.ds(k * rows, rows), pl.ds(64 + k * rows, rows)
            first.append(
                (
                    links.copy(grad_out.at[a], fwd.at[0, a], yp),
                    links.copy(grad_out.at[b], fwd.at[1, a], ym),
                )
            )
        sib_waits.append(links.copy(grad_out, tg.at[t], sib))
        yield
        second = []
        from_below = lax.div(wrap(y - 1, NY), 2) * 2 + core
        from_above = lax.div(wrap(y + 1, NY), 2) * 2 + core
        for k in range(n_pieces):
            a, b = pl.ds(k * rows, rows), pl.ds(64 + k * rows, rows)
            first[k][0].wait_recv()
            u = links.copy(fwd.at[0, a], tg.at[from_below, a], yp)
            first[k][1].wait_recv()
            second.append((u, links.copy(fwd.at[1, a], tg.at[from_above, b], ym)))
            yield
        for k in range(n_pieces):
            a, b = pl.ds(k * rows, rows), pl.ds(64 + k * rows, rows)
            second[k][0].wait_recv()
            sib_waits.append(links.copy(tg.at[partner, a], tg.at[partner, a], sib))
            second[k][1].wait_recv()
            sib_waits.append(links.copy(tg.at[partner, b], tg.at[partner, b], sib))
            yield
        for c in sib_waits:
            c.wait_recv()

    def w_out_stream(part):
        hs = pl.ds(64 * part, 64)
        c = links.copy(wv.at[x, yl, z, hs], wv.at[x, yl, z, hs], pair)
        yield
        c.wait_recv()
        if part == 0:
            yield from ring_gather(links, NX, x, lambda i: wv.at[i, :, z, hs], 1, xp, xm)
            yield from ring_gather(links, NZ, z, lambda i: wv.at[:, :, i, hs], 2, zp, zm)
        else:
            yield from ring_gather(links, NZ, z, lambda i: wv.at[x, :, i, hs], 1, zp, zm)
            yield from ring_gather(links, NX, x, lambda i: wv.at[i, :, :, hs], 1, xp, xm)

    q_waits = []

    def w_query_stream(part):
        hs = pl.ds(128 * part, 128)

        def hand_over(piece):
            q_waits.append(links.copy(piece, piece, sib))

        yield from ring_gather(links, NY, y, lambda i: qv.at[core, x, i, z, hs], 64, yp, ym)
        if part == 0:
            yield from ring_gather(links, NX, x, lambda i: qv.at[core, i, :, z, hs], 2, xp, xm)
            yield from ring_gather(
                links, NZ, z, lambda i: qv.at[core, :, :, i, hs], 2, zp, zm, hand_over
            )
        else:
            yield from ring_gather(links, NZ, z, lambda i: qv.at[core, x, :, i, hs], 2, zp, zm)
            yield from ring_gather(
                links, NX, x, lambda i: qv.at[core, i, :, :, hs], 2, xp, xm, hand_over
            )

    live = {}

    def go(*names):
        for name in names:
            if name in live:
                try:
                    next(live[name])
                except StopIteration:
                    del live[name]

    def finish(*names):
        while any(name in live for name in names):
            go(*names)

    local[0].wait()
    local[1].wait()
    live["wa"], live["wb"] = w_out_stream(0), w_out_stream(1)
    live["qa"], live["qb"] = w_query_stream(0), w_query_stream(1)
    live["g"] = grads_stream()
    go("wa", "wb", "qa", "qb", "g")
    halo_copies = [
        links.copy(keys.at[0:SPAN], halo.at[0, 0], rp),
        links.copy(values.at[0:SPAN], halo.at[0, 1], rp),
        links.copy(keys.at[SPAN : 2 * SPAN], halo.at[1, 0], rm),
        links.copy(values.at[SPAN : 2 * SPAN], halo.at[1, 1], rm),
    ]
    go("wa", "wb", "qa", "qb")
    go("wa", "wb")
    go("wa", "wb", "g", "qa", "qb")
    go("wa", "wb", "qa", "qb", "g")
    go("wa", "wb", "qb", "g")
    while "wa" in live or "wb" in live or "g" in live:
        go("wa", "wb", "g", "qb", "qa")
    for c in local[2:]:
        c.wait()
    for c in halo_copies:
        c.wait_recv()

    half_width = 4 * HD

    def dw_step(j, carry):
        at = pl.ds(pl.multiple_of(j * half_width, half_width), half_width)
        lhs = tg[:, :, at].reshape(2 * SPAN, half_width)
        part = jnp.dot(att_t[...], lhs, preferred_element_type=F32).astype(BF)
        xi, rest = lax.div(j, 4), lax.rem(j, 4)
        yi, zi = lax.div(rest, 2), lax.rem(rest, 2) * 4
        for q in range(4):
            pb[xi, yi, zi + q] = part[:, q * HD : (q + 1) * HD]
        return carry

    lax.fori_loop(0, 16, dw_step, 0)

    lo, hi = pl.ds(0, HD), pl.ds(HD, HD)

    def reduce_a():
        yield from ring_reduce(links, NZ, z, lambda i: pb.at[:, :, i, lo], raz, 2, zp, zm)
        yield from ring_reduce(links, NX, x, lambda i: pb.at[i, :, z, lo], rax, 1, xp, xm)
        c = links.copy(pb.at[x, 1 - yl, z, lo], ray, pair)
        yield
        c.wait_recv()
        total = pb[x, yl, z, lo].astype(F32) + ray[...].astype(F32)
        dwo[:, 0:HD] = total.T

    def reduce_b():
        yield from ring_reduce(links, NX, x, lambda i: pb.at[i, :, :, hi], rbx, 1, xp, xm)
        yield from ring_reduce(links, NZ, z, lambda i: pb.at[x, :, i, hi], rbz, 1, zp, zm)
        c = links.copy(pb.at[x, 1 - yl, z, hi], rby, pair)
        yield
        c.wait_recv()
        total = pb[x, yl, z, hi].astype(F32) + rby[...].astype(F32)
        dwo[:, HD : 2 * HD] = total.T

    live["ra"], live["rb"] = reduce_a(), reduce_b()
    go("ra", "rb")

    acc[...] = jnp.zeros_like(acc)

    def ag_step(j, carry):
        at = pl.ds(pl.multiple_of(j * half_width, half_width), half_width)
        lhs = tg[:, :, at].reshape(2 * SPAN, half_width)
        xi, rest = lax.div(j, 4), lax.rem(j, 4)
        yi, zi = lax.div(rest, 2), lax.rem(rest, 2) * 4
        rhs = wv[xi, yi, pl.ds(zi, 4)].reshape(half_width, 2 * HD)
        acc[...] += jnp.dot(lhs, rhs, preferred_element_type=F32)
        return carry

    lax.fori_loop(0, 16, ag_step, 0)
    ag[...] = acc[...].astype(BF)
    go("ra", "rb")

    last = r == n_ctx - 1
    inv_root = 1.0 / math.sqrt(HD)
    row_at = lax.broadcasted_iota(jnp.int32, (SPAN, SPAN), 0)
    col_at = lax.broadcasted_iota(jnp.int32, (SPAN, SPAN), 1)
    eye = row_at == col_at
    q_at = lax.broadcasted_iota(jnp.int32, (SPAN, 2 * SPAN), 0)
    k_at = lax.broadcasted_iota(jnp.int32, (SPAN, 2 * SPAN), 1) - SPAN

    def column(row, zero):
        return jnp.sum(jnp.where(eye, row, zero), axis=1, keepdims=True)

    def seg_of(span):
        return seg[:, pl.ds(pl.multiple_of(span * SPAN, SPAN), SPAN)]

    def unit(b, h):
        rows_b, cols_h = pl.ds(b * SPAN, SPAN), pl.ds(h * HD, HD)
        span = r if b == 0 else 2 * n_ctx - 1 - r
        seg_q = seg_of(span)
        seg_k = jnp.concatenate([seg_of(jnp.maximum(span - 1, 0)), seg_q], axis=1)
        allowed = (
            (k_at <= q_at)
            & (k_at + span * SPAN >= 0)
            & (seg_k == column(seg_q, 0))
        )
        prev_k, prev_v = halo[b, 0], halo[b, 1]
        if b == 1:
            prev_k = jnp.where(last, keys[0:SPAN], prev_k)
            prev_v = jnp.where(last, values[0:SPAN], prev_v)
        k_cat = jnp.concatenate([prev_k, keys[rows_b]], axis=0)
        v_cat = jnp.concatenate([prev_v, values[rows_b]], axis=0)
        qb, db = queries[rows_b, cols_h], ag[rows_b, cols_h]
        delta = jnp.sum(
            db.astype(F32) * attended[rows_b, cols_h].astype(F32), axis=1, keepdims=True
        )
        lse = column(log_sums[h : h + 1, rows_b], 0.0)
        scores = contract(qb, k_cat, 1, 1) * inv_root
        prob = jnp.where(allowed, jnp.exp(scores - lse), 0.0)
        dprob = contract(db, v_cat, 1, 1)
        dscore = (prob * (dprob - delta)).astype(BF)
        dq = jnp.dot(dscore, k_cat, preferred_element_type=F32) * inv_root
        qkv[rows_b, cols_h] = dq.astype(BF)
        kg = contract(dscore, qb, 0, 0) * inv_root
        vg = contract(prob.astype(BF), db, 0, 0)
        if h == 0:
            kvg[b, :, 0:HD] = kg
            kvg[b, :, HD : 2 * HD] = vg
        else:
            kvg[b, :, 0:HD] += kg
            kvg[b, :, HD : 2 * HD] += vg

    for b in range(2):
        for h in range(2):
            unit(b, h)
            go("ra", "rb")

    kvback[0] = kvg[0, 0:SPAN].astype(BF)
    kvback[1] = jnp.where(last, 0.0, kvg[1, 0:SPAN]).astype(BF)
    to_left = links.copy(kvback.at[0], kvland.at[0], rm)
    to_right = links.copy(kvback.at[1], kvland.at[1], rp)
    to_left.wait_recv()
    to_right.wait_recv()
    low = (
        kvg[0, SPAN : 2 * SPAN]
        + jnp.where(last, kvg[1, 0:SPAN], 0.0)
        + kvland[0].astype(F32)
    )
    high = kvg[1, SPAN : 2 * SPAN] + kvland[1].astype(F32)
    qkv[0:SPAN, 2 * HD : 4 * HD] = low.astype(BF)
    qkv[SPAN : 2 * SPAN, 2 * HD : 4 * HD] = high.astype(BF)

    def rows_of(d):
        return pl.ds(pl.multiple_of(d * HD, HD), HD)

    sib_t, far_sib_t = 2 * yh + other, 2 * (1 - yh) + other
    swaps = [
        links.copy(qkv.at[rows_of(partner)], ab.at[t], far),
        links.copy(qkv.at[rows_of(far_sib_t)], ab.at[t], far_sib),
        links.copy(qkv.at[rows_of(sib_t)], ab.at[t], sib),
    ]
    ab[t] = qkv[rows_of(t)]
    finish("ra", "rb")
    finish("qa", "qb")
    for c in swaps:
        c.wait_recv()
    for c in q_waits:
        c.wait_recv()

    kv_sum = jnp.sum(ab[:, :, 2 * HD : 4 * HD].astype(F32), axis=0).astype(BF)

    def out_step(j, carry):
        xi, yi = lax.div(j, 2), lax.rem(j, 2)
        for q in range(4):
            at = pl.ds(pl.multiple_of(j * (NZ * HD) + q * 2 * HD, 2 * HD), 2 * HD)
            total = jnp.dot(kv_sum, kvw[:, at], preferred_element_type=F32)
            for g in range(4):
                rhs = jnp.concatenate(
                    [
                        qv[g % 2, xi, 2 * (g // 2) + yi, 2 * q],
                        qv[g % 2, xi, 2 * (g // 2) + yi, 2 * q + 1],
                    ],
                    axis=1,
                )
                total += jnp.dot(ab[g, :, 0 : 2 * HD], rhs, preferred_element_type=F32)
            gin[:, at] = total.astype(BF)
        return carry

    lax.fori_loop(0, 8, out_step, 0)
    for c in links.started:
        c.wait_send()


def on_device(
    grad_out, queries, attended, keys, values, log_sums, segment_ids, w_out, w_query, w_key, w_value
):
    vmem = pl.BlockSpec(memory_space=pltpu.VMEM)
    hbm = pl.BlockSpec(memory_space=pl.ANY)
    own, model = grad_out.shape
    blocks = (NX, 2, NZ)
    return pl.pallas_call(
        kernel,
        out_shape=(
            jax.ShapeDtypeStruct((own, model), BF),
            jax.ShapeDtypeStruct((HD, 2 * HD), F32),
        ),
        in_specs=[hbm] + [vmem] * 6 + [hbm] * 4,
        out_specs=(vmem, vmem),
        scratch_shapes=[
            pltpu.VMEM((4, own, model), BF),
            pltpu.VMEM((2, 64, model), BF),
            pltpu.VMEM(blocks + (HD, 2 * HD), BF),
            pltpu.VMEM((2, NX, NY, NZ, 2 * HD, HD), BF),
            pltpu.VMEM((2 * HD, model), BF),
            pltpu.VMEM(blocks + (2 * HD, HD), BF),
            pltpu.VMEM((2, 4, NX, 2, HD, HD), BF),
            pltpu.VMEM((2, 2, 2, HD, HD), BF),
            pltpu.VMEM((HD, HD), BF),
            pltpu.VMEM((2, 2, 2, NZ, HD, HD), BF),
            pltpu.VMEM((2, 4, 2, HD, HD), BF),
            pltpu.VMEM((HD, HD), BF),
            pltpu.VMEM((2, 2, SPAN, HD), BF),
            pltpu.VMEM((2 * SPAN, 2 * HD), BF),
            pltpu.VMEM((2 * HD, 2 * SPAN), BF),
            pltpu.VMEM((2 * SPAN, 2 * HD), F32),
            pltpu.VMEM((2 * SPAN, 4 * HD), BF),
            pltpu.VMEM((2, 2 * SPAN, 2 * HD), F32),
            pltpu.VMEM((2, SPAN, 2 * HD), BF),
            pltpu.VMEM((2, SPAN, 2 * HD), BF),
            pltpu.VMEM((4, HD, 4 * HD), BF),
            pltpu.SemaphoreType.DMA((N_REMOTE,)),
            pltpu.SemaphoreType.DMA((N_REMOTE,)),
            pltpu.SemaphoreType.DMA((N_LOCAL,)),
        ],
        compiler_params=pltpu.CompilerParams(
            collective_id=0, has_side_effects=True, vmem_limit_bytes=60 * 2**20
        ),
    )(
        grad_out, queries, attended, keys, values, log_sums, segment_ids, w_out, w_query, w_key, w_value
    )


def solution(mesh):
    placed = (
        P(("dp", "context", "tensor"), None),
        P(("dp", "context"), "tensor"),
        P(("dp", "context"), "tensor"),
        P(("dp", "context"), None),
        P(("dp", "context"), None),
        P("tensor", ("dp", "context")),
        P("dp", None),
        P(("dp", "context"), "tensor"),
        P("tensor", ("dp", "context")),
        P(),
        P(),
    )
    return jax.shard_map(
        on_device,
        mesh=mesh,
        in_specs=placed,
        out_specs=(P(("dp", "context", "tensor"), None), P(("dp", "context"), "tensor")),
        check_vma=False,
    )
```

```python
import functools
import math

import jax
import jax.numpy as jnp
from jax import lax
from jax.experimental import pallas as pl
from jax.experimental.pallas import tpu as pltpu
from jax.sharding import PartitionSpec as P

MESH = pl.DeviceIdType.MESH
BF = jnp.bfloat16
F32 = jnp.float32
NX, NY, NZ = 4, 4, 8
SPAN = 256
HD = 128
N_REMOTE = 200
N_LOCAL = 8
WINDOW = 2
W_ROWS = 64
Q_ROWS = ((0, 48), (48, 96), (144, 112))
ORDER = (
    "gvwqrssqsrvwsqwsvrggvsgrsvwvrgggrgghabqr",
    "wahhbhqavhhhwhhcdsaqbcwbdvtttttcbaqrsabd",
    "btdcqrdsdcdtcypppyp",
)


def wrap(i, n):
    return lax.rem(i + n, n)


class Links:
    def __init__(self, send, recv):
        self.send, self.recv, self.started = send, recv, []

    def copy(self, src, dst, dev):
        n = len(self.started)
        c = pltpu.make_async_remote_copy(
            src_ref=src,
            dst_ref=dst,
            send_sem=self.send.at[n],
            recv_sem=self.recv.at[n],
            device_id=dev,
            device_id_type=MESH,
        )
        c.start()
        self.started.append(c)
        return c


def ring_gather(links, n, i, slab, half, up, down, arrived=None):
    k = n // 2
    cp = links.copy(slab(i), slab(i), up)
    cm = links.copy(slab(i), slab(i), down)
    if arrived is not None:
        arrived(slab(i))
    for s in range(1, k):
        yield
        before, after = slab(wrap(i - s, n)), slab(wrap(i + s, n))
        cp.wait_recv()
        piece = before if s < k - 1 or half is None else before.at[0:half]
        cp = links.copy(piece, piece, up)
        if arrived is not None:
            arrived(before)
        cm.wait_recv()
        if s < k - 1:
            cm = links.copy(after, after, down)
        elif half is not None:
            piece = after.at[half : 2 * half]
            cm = links.copy(piece, piece, down)
        else:
            cm = None
        if arrived is not None:
            arrived(after)
    yield
    cp.wait_recv()
    if cm is not None:
        cm.wait_recv()
    if arrived is not None:
        arrived(slab(wrap(i + k, n)))


def spread(links, piece, devs):
    copies = [links.copy(piece, piece, d) for d in devs]
    yield
    for c in copies:
        c.wait_recv()


def ring_reduce(links, n, i, slab, buf, half, up, down):
    k = n // 2
    far = wrap(i + k, n)
    cp = links.copy(slab(far).at[0:half], buf.at[0, 0, 0:half], up)
    cm = links.copy(slab(far).at[half : 2 * half], buf.at[1, 0, half : 2 * half], down)
    yield

    def add(dst, part):
        dst[...] = (dst[...].astype(F32) + part[...].astype(F32)).astype(BF)

    for step in range(1, k):
        s = k - step
        dst = slab(wrap(i + s, n))
        cp.wait_recv()
        if step == 1:
            add(dst.at[0:half], buf.at[0, 0, 0:half])
        else:
            add(dst, buf.at[0, step - 1])
        cp = links.copy(dst, buf.at[0, step], up)
        dst = slab(wrap(i - s, n))
        cm.wait_recv()
        if step == 1:
            add(dst.at[half : 2 * half], buf.at[1, 0, half : 2 * half])
        else:
            add(dst, buf.at[1, step - 1])
        cm = links.copy(dst, buf.at[1, step], down)
        yield
    cp.wait_recv()
    cm.wait_recv()
    dst = slab(i)
    dst[...] = (
        dst[...].astype(F32) + buf[0, k - 1].astype(F32) + buf[1, k - 1].astype(F32)
    ).astype(BF)


def spread_reduce(links, n, i, slab, buf, devs):
    copies = [
        links.copy(slab(wrap(i + step, n)), buf.at[j], d)
        for j, (step, d) in enumerate(zip((1, n - 1, 2), devs))
    ]
    yield
    for c in copies:
        c.wait_recv()
    dst = slab(i)
    total = dst[...].astype(F32)
    for j in range(3):
        total += buf[j].astype(F32)
    dst[...] = total.astype(BF)


def contract(a, b, da, db):
    return lax.dot_general(a, b, (((da,), (db,)), ((), ())), preferred_element_type=F32)


def kernel(
    grad_out, queries, attended, keys, values, log_sums, seg, w_out, w_query, w_key, w_value,
    gin, dwo,
    tg, wv, qv, kvw, pb, raz, rax, rbx, rbz, ry,
    halo, ag, att_t, acc, qkv, kvg, kvback, kvland, ab, send, recv, loc,
):
    x = lax.axis_index("dp")
    r = lax.axis_index("context")
    t = lax.axis_index("tensor")
    yl, z = lax.div(r, NZ), lax.rem(r, NZ)
    yh, core = lax.div(t, 2), lax.rem(t, 2)
    y = 2 * yh + yl
    other = 1 - core
    partner = 2 * (1 - yh) + core

    def dev(x, y, z, core):
        return {
            "dp": x,
            "context": lax.rem(y, 2) * NZ + z,
            "tensor": lax.div(y, 2) * 2 + core,
        }

    xp, xm = dev(wrap(x + 1, NX), y, z, core), dev(wrap(x - 1, NX), y, z, core)
    yp, ym = dev(x, wrap(y + 1, NY), z, core), dev(x, wrap(y - 1, NY), z, core)
    zp, zm = dev(x, y, wrap(z + 1, NZ), core), dev(x, y, wrap(z - 1, NZ), core)
    pair = dev(x, 2 * yh + 1 - yl, z, core)
    sib = dev(x, y, z, other)
    far = dev(x, wrap(y + 2, NY), z, core)
    far_x = dev(wrap(x + 2, NX), y, z, core)
    far_sib = dev(x, wrap(y + 2, NY), z, other)
    n_ctx = 2 * NZ
    rp = {"dp": x, "context": wrap(r + 1, n_ctx), "tensor": t}
    rm = {"dp": x, "context": wrap(r - 1, n_ctx), "tensor": t}
    links = Links(send, recv)

    local = [
        pltpu.make_async_copy(w_out, wv.at[x, yl, z], loc.at[0]),
        pltpu.make_async_copy(w_query, qv.at[core, x, y, z], loc.at[1]),
        pltpu.make_async_copy(grad_out, tg.at[t], loc.at[2]),
        pltpu.make_async_copy(w_key, kvw.at[0:HD], loc.at[3]),
        pltpu.make_async_copy(w_value, kvw.at[HD : 2 * HD], loc.at[4]),
    ]
    for c in local:
        c.start()
    partners = (xp, xm, yp, ym, zp, zm, rp, rm, sib, far, far_sib, far_x)
    barrier = pltpu.get_barrier_semaphore()
    for d in partners:
        pl.semaphore_signal(barrier, inc=1, device_id=d, device_id_type=MESH)
    att_t[...] = attended[...].astype(F32).T.astype(BF)
    pl.semaphore_wait(barrier, len(partners))

    halo_copies = [
        links.copy(keys.at[0:SPAN], halo.at[0, 0], rp),
        links.copy(values.at[0:SPAN], halo.at[0, 1], rp),
        links.copy(keys.at[SPAN : 2 * SPAN], halo.at[1, 0], rm),
        links.copy(values.at[SPAN : 2 * SPAN], halo.at[1, 1], rm),
    ]
    chunk = NZ * HD
    n_chunks = 2 * NX
    far_copies, own_copy, sib_copies = [], [], []

    def cols(j):
        return pl.ds(((j % NX) * 2 + j // NX) * chunk, chunk)

    def send_far():
        j = len(far_copies)
        if j < n_chunks:
            far_copies.append(links.copy(grad_out.at[:, cols(j)], tg.at[t, :, cols(j)], far))

    def dw_chunk(j):
        if j == 0:
            local[2].wait()
            own_copy[0].wait_recv()
        sib_copies[j].wait_recv()
        xi, yi = j % NX, j // NX

        def step(q, carry):
            at = pl.ds(pl.multiple_of((xi * 2 + yi) * chunk + q * 4 * HD, 4 * HD), 4 * HD)
            lhs = tg[:, :, at].reshape(2 * SPAN, 4 * HD)
            part = jnp.dot(att_t[...], lhs, preferred_element_type=F32).astype(BF)
            for u in range(4):
                pb[xi, yi, 4 * q + u] = part[:, u * HD : (u + 1) * HD]
            return carry

        lax.fori_loop(0, 2, step, 0)

    def grads_stream(first):
        yield
        if first == 0:
            for _ in range(WINDOW):
                send_far()
            own_copy.append(links.copy(grad_out, tg.at[t], sib))
        for j in range(first, first + NX):
            yield
            far_copies[j].wait_recv()
            send_far()
            got = tg.at[partner, :, cols(j)]
            sib_copies.append(links.copy(got, got, sib))
            if j > first:
                yield
                dw_chunk(j - 1)
        yield
        dw_chunk(first + NX - 1)

    def w_out_stream(part):
        hs = pl.ds(0, W_ROWS) if part == 0 else pl.ds(W_ROWS, HD - W_ROWS)
        yield
        c = links.copy(wv.at[x, yl, z, hs], wv.at[x, yl, z, hs], pair)
        yield
        c.wait_recv()
        if part == 0:
            yield from spread(links, wv.at[x, :, z, hs], (xp, xm, far_x))
            yield from ring_gather(links, NZ, z, lambda i: wv.at[:, :, i, hs], 2, zp, zm)
        else:
            yield from ring_gather(links, NZ, z, lambda i: wv.at[x, :, i, hs], 1, zp, zm)
            yield from ring_gather(links, NX, x, lambda i: wv.at[i, :, :, hs], 1, xp, xm)

    q_waits = []

    def w_query_stream(part):
        lo_row, n_rows = Q_ROWS[part]
        hs = pl.ds(lo_row, n_rows)

        def hand_over(piece):
            q_waits.append(links.copy(piece, piece, sib))

        yield
        if part == 2:
            yield from ring_gather(links, NZ, z, lambda i: qv.at[core, x, y, i, hs], None, zp, zm)
            yield from ring_gather(links, NX, x, lambda i: qv.at[core, i, y, :, hs], 4, xp, xm)
            yield
            yield from ring_gather(
                links, NY, y, lambda i: qv.at[core, :, i, :, hs], 2, yp, ym, hand_over
            )
            return
        yield from spread(links, qv.at[core, x, y, z, hs], (yp, ym, far))
        if part == 0:
            yield from spread(links, qv.at[core, x, :, z, hs], (xp, xm, far_x))
            yield
            yield from ring_gather(
                links, NZ, z, lambda i: qv.at[core, :, :, i, hs], 2, zp, zm, hand_over
            )
        else:
            yield from ring_gather(links, NZ, z, lambda i: qv.at[core, x, :, i, hs], 2, zp, zm)
            yield
            yield from ring_gather(
                links, NX, x, lambda i: qv.at[core, i, :, :, hs], 2, xp, xm, hand_over
            )

    lo, hi = pl.ds(0, HD), pl.ds(HD, HD)

    def reduce_a(yi):
        yield
        yield from ring_reduce(
            links, NZ, z, lambda i: pb.at[:, yi, i, lo], raz.at[yi], 2, zp, zm
        )
        yield from spread_reduce(
            links, NX, x, lambda i: pb.at[i, yi, z, lo], rax.at[yi], (xp, xm, far_x)
        )

    def reduce_b(yi):
        yield
        yield from ring_reduce(
            links, NX, x, lambda i: pb.at[i, yi, :, hi], rbx.at[yi], 4, xp, xm
        )
        yield from ring_reduce(
            links, NZ, z, lambda i: pb.at[x, yi, i, hi], rbz.at[yi], 64, zp, zm
        )

    def pair_sum():
        yield
        c = links.copy(pb.at[x, 1 - yl, z], ry, pair)
        yield
        c.wait_recv()
        dwo[...] = (pb[x, yl, z].astype(F32) + ry[...].astype(F32)).T

    def ag_steps(first):
        def step(j, carry):
            at = pl.ds(pl.multiple_of(j * 4 * HD, 4 * HD), 4 * HD)
            lhs = tg[:, :, at].reshape(2 * SPAN, 4 * HD)
            xi, rest = lax.div(j, 4), lax.rem(j, 4)
            yi, zi = lax.div(rest, 2), lax.rem(rest, 2) * 4
            rhs = wv[xi, yi, pl.ds(zi, 4)].reshape(4 * HD, 2 * HD)
            acc[...] += jnp.dot(lhs, rhs, preferred_element_type=F32)
            return carry

        lax.fori_loop(first, first + 4, step, 0)

    last = r == n_ctx - 1
    inv_root = 1.0 / math.sqrt(HD)
    row_at = lax.broadcasted_iota(jnp.int32, (SPAN, SPAN), 0)
    col_at = lax.broadcasted_iota(jnp.int32, (SPAN, SPAN), 1)
    eye = row_at == col_at
    q_at = lax.broadcasted_iota(jnp.int32, (SPAN, 2 * SPAN), 0)
    k_at = lax.broadcasted_iota(jnp.int32, (SPAN, 2 * SPAN), 1) - SPAN

    def column(row, zero):
        return jnp.sum(jnp.where(eye, row, zero), axis=1, keepdims=True)

    def seg_of(span):
        return seg[:, pl.ds(pl.multiple_of(span * SPAN, SPAN), SPAN)]

    def unit(b, h):
        rows_b, cols_h = pl.ds(b * SPAN, SPAN), pl.ds(h * HD, HD)
        span = r if b == 0 else 2 * n_ctx - 1 - r
        seg_q = seg_of(span)
        seg_k = jnp.concatenate([seg_of(jnp.maximum(span - 1, 0)), seg_q], axis=1)
        allowed = (
            (k_at <= q_at)
            & (k_at + span * SPAN >= 0)
            & (seg_k == column(seg_q, 0))
        )
        prev_k, prev_v = halo[b, 0], halo[b, 1]
        if b == 1:
            prev_k = jnp.where(last, keys[0:SPAN], prev_k)
            prev_v = jnp.where(last, values[0:SPAN], prev_v)
        k_cat = jnp.concatenate([prev_k, keys[rows_b]], axis=0)
        v_cat = jnp.concatenate([prev_v, values[rows_b]], axis=0)
        qb, db = queries[rows_b, cols_h], ag[rows_b, cols_h]
        delta = jnp.sum(
            db.astype(F32) * attended[rows_b, cols_h].astype(F32), axis=1, keepdims=True
        )
        lse = column(log_sums[h : h + 1, rows_b], 0.0)
        scores = contract(qb, k_cat, 1, 1) * inv_root
        prob = jnp.where(allowed, jnp.exp(scores - lse), 0.0)
        dprob = contract(db, v_cat, 1, 1)
        dscore = (prob * (dprob - delta)).astype(BF)
        dq = jnp.dot(dscore, k_cat, preferred_element_type=F32) * inv_root
        qkv[rows_b, cols_h] = dq.astype(BF)
        kg = contract(dscore, qb, 0, 0) * inv_root
        vg = contract(prob.astype(BF), db, 0, 0)
        if h == 0:
            kvg[b, :, 0:HD] = kg
            kvg[b, :, HD : 2 * HD] = vg
        else:
            kvg[b, :, 0:HD] += kg
            kvg[b, :, HD : 2 * HD] += vg

    def rows_of(d):
        return pl.ds(pl.multiple_of(d * HD, HD), HD)

    def attention_stream():
        for part in range(4):
            yield
            if part == 0:
                acc[...] = jnp.zeros_like(acc)
            ag_steps(4 * part)
        yield
        ag[...] = acc[...].astype(BF)
        for c in halo_copies:
            c.wait_recv()
        for b in range(2):
            for h in range(2):
                unit(b, h)
        kvback[0] = kvg[0, 0:SPAN].astype(BF)
        kvback[1] = jnp.where(last, 0.0, kvg[1, 0:SPAN]).astype(BF)
        to_left = links.copy(kvback.at[0], kvland.at[0], rm)
        to_right = links.copy(kvback.at[1], kvland.at[1], rp)
        yield
        to_left.wait_recv()
        to_right.wait_recv()
        low = (
            kvg[0, SPAN : 2 * SPAN]
            + jnp.where(last, kvg[1, 0:SPAN], 0.0)
            + kvland[0].astype(F32)
        )
        high = kvg[1, SPAN : 2 * SPAN] + kvland[1].astype(F32)
        qkv[0:SPAN, 2 * HD : 4 * HD] = low.astype(BF)
        qkv[SPAN : 2 * SPAN, 2 * HD : 4 * HD] = high.astype(BF)
        swaps = [
            links.copy(qkv.at[rows_of(partner)], ab.at[t], far),
            links.copy(qkv.at[rows_of(2 * (1 - yh) + other)], ab.at[t], far_sib),
            links.copy(qkv.at[rows_of(2 * yh + other)], ab.at[t], sib),
        ]
        ab[t] = qkv[rows_of(t)]
        yield
        for c in swaps:
            c.wait_recv()

    def out_stream():
        yield
        local[3].wait()
        local[4].wait()
        for c in q_waits:
            c.wait_recv()
        kv_sum = jnp.sum(ab[:, :, 2 * HD : 4 * HD].astype(F32), axis=0).astype(BF)

        def step(j, carry):
            xi, yi = lax.div(j, 2), lax.rem(j, 2)
            for q in range(4):
                at = pl.ds(pl.multiple_of(j * chunk + q * 2 * HD, 2 * HD), 2 * HD)
                total = jnp.dot(kv_sum, kvw[:, at], preferred_element_type=F32)
                for g in range(4):
                    heads = qv.at[g % 2, xi, 2 * (g // 2) + yi]
                    rhs = jnp.concatenate([heads[2 * q], heads[2 * q + 1]], axis=1)
                    total += jnp.dot(ab[g, :, 0 : 2 * HD], rhs, preferred_element_type=F32)
                gin[:, at] = total.astype(BF)
            return carry

        for part in range(4):
            lax.fori_loop(2 * part, 2 * part + 2, step, 0)
            if part < 3:
                yield

    local[0].wait()
    local[1].wait()
    live = {
        "w": w_out_stream(0),
        "v": w_out_stream(1),
        "g": grads_stream(0),
        "h": grads_stream(NX),
        "q": w_query_stream(0),
        "r": w_query_stream(1),
        "s": w_query_stream(2),
        "a": reduce_a(0),
        "b": reduce_b(0),
        "c": reduce_a(1),
        "d": reduce_b(1),
        "y": pair_sum(),
        "t": attention_stream(),
        "p": out_stream(),
    }
    for stream in live.values():
        next(stream)
    for name in "".join(ORDER):
        next(live[name], 0)
    for stream in live.values():
        assert next(stream, 0) == 0
    for c in links.started:
        c.wait_send()


def on_device(
    grad_out, queries, attended, keys, values, log_sums, segment_ids, w_out, w_query, w_key, w_value
):
    vmem = pl.BlockSpec(memory_space=pltpu.VMEM)
    hbm = pl.BlockSpec(memory_space=pl.ANY)
    own, model = grad_out.shape
    blocks = (NX, 2, NZ)
    return pl.pallas_call(
        kernel,
        out_shape=(
            jax.ShapeDtypeStruct((own, model), BF),
            jax.ShapeDtypeStruct((HD, 2 * HD), F32),
        ),
        in_specs=[hbm] + [vmem] * 6 + [hbm] * 4,
        out_specs=(vmem, vmem),
        scratch_shapes=[
            pltpu.VMEM((4, own, model), BF),
            pltpu.VMEM(blocks + (HD, 2 * HD), BF),
            pltpu.VMEM((2, NX, NY, NZ, 2 * HD, HD), BF),
            pltpu.VMEM((2 * HD, model), BF),
            pltpu.VMEM(blocks + (2 * HD, HD), BF),
            pltpu.VMEM((2, 2, 4, NX, HD, HD), BF),
            pltpu.VMEM((2, 3, HD, HD), BF),
            pltpu.VMEM((2, 2, 2, NZ, HD, HD), BF),
            pltpu.VMEM((2, 2, 4, HD, HD), BF),
            pltpu.VMEM((2 * HD, HD), BF),
            pltpu.VMEM((2, 2, SPAN, HD), BF),
            pltpu.VMEM((2 * SPAN, 2 * HD), BF),
            pltpu.VMEM((2 * HD, 2 * SPAN), BF),
            pltpu.VMEM((2 * SPAN, 2 * HD), F32),
            pltpu.VMEM((2 * SPAN, 4 * HD), BF),
            pltpu.VMEM((2, 2 * SPAN, 2 * HD), F32),
            pltpu.VMEM((2, SPAN, 2 * HD), BF),
            pltpu.VMEM((2, SPAN, 2 * HD), BF),
            pltpu.VMEM((4, HD, 4 * HD), BF),
            pltpu.SemaphoreType.DMA((N_REMOTE,)),
            pltpu.SemaphoreType.DMA((N_REMOTE,)),
            pltpu.SemaphoreType.DMA((N_LOCAL,)),
        ],
        compiler_params=pltpu.CompilerParams(
            collective_id=0, has_side_effects=True, vmem_limit_bytes=52 * 2**20
        ),
    )(
        grad_out, queries, attended, keys, values, log_sums, segment_ids, w_out, w_query, w_key, w_value
    )


def solution(mesh):
    placed = (
        P(("dp", "context", "tensor"), None),
        P(("dp", "context"), "tensor"),
        P(("dp", "context"), "tensor"),
        P(("dp", "context"), None),
        P(("dp", "context"), None),
        P("tensor", ("dp", "context")),
        P("dp", None),
        P(("dp", "context"), "tensor"),
        P("tensor", ("dp", "context")),
        P(),
        P(),
    )
    return jax.shard_map(
        on_device,
        mesh=mesh,
        in_specs=placed,
        out_specs=(P(("dp", "context", "tensor"), None), P(("dp", "context"), "tensor")),
        check_vma=False,
    )
```

```python
import functools
import math

import jax
import jax.numpy as jnp
from jax import lax
from jax.experimental import pallas as pl
from jax.experimental.pallas import tpu as pltpu
from jax.sharding import PartitionSpec as P

MESH = pl.DeviceIdType.MESH
BF = jnp.bfloat16
F32 = jnp.float32
NX, NY, NZ = 4, 4, 8
SPAN = 256
HD = 128
N_REMOTE = 200
N_LOCAL = 8
WINDOW = 8
W_ROWS = 64
Q_ROWS = ((0, 48), (48, 112), (160, 96))
ORDER = (
    "svqrwgvswvssvqgrsvwvrsgwqggrggggbavhwbrs",
    "qswhhrrqhhvhwabhhtqhtcbatttqcdsdbtarcqdd",
    "casdbcrdtbacdyppppy",
)


def wrap(i, n):
    return lax.rem(i + n, n)


class Links:
    def __init__(self, send, recv):
        self.send, self.recv, self.started = send, recv, []

    def copy(self, src, dst, dev):
        n = len(self.started)
        c = pltpu.make_async_remote_copy(
            src_ref=src,
            dst_ref=dst,
            send_sem=self.send.at[n],
            recv_sem=self.recv.at[n],
            device_id=dev,
            device_id_type=MESH,
        )
        c.start()
        self.started.append(c)
        return c


def ring_gather(links, n, i, slab, half, up, down, arrived=None):
    k = n // 2
    cp = links.copy(slab(i), slab(i), up)
    cm = links.copy(slab(i), slab(i), down)
    if arrived is not None:
        arrived(slab(i))
    for s in range(1, k):
        yield
        before, after = slab(wrap(i - s, n)), slab(wrap(i + s, n))
        cp.wait_recv()
        piece = before if s < k - 1 or half is None else before.at[0:half]
        cp = links.copy(piece, piece, up)
        if arrived is not None:
            arrived(before)
        cm.wait_recv()
        if s < k - 1:
            cm = links.copy(after, after, down)
        elif half is not None:
            piece = after.at[half : 2 * half]
            cm = links.copy(piece, piece, down)
        else:
            cm = None
        if arrived is not None:
            arrived(after)
    yield
    cp.wait_recv()
    if cm is not None:
        cm.wait_recv()
    if arrived is not None:
        arrived(slab(wrap(i + k, n)))


def spread(links, piece, devs):
    copies = [links.copy(piece, piece, d) for d in devs]
    yield
    for c in copies:
        c.wait_recv()


def ring_reduce(links, n, i, slab, buf, half, up, down):
    k = n // 2
    far = wrap(i + k, n)
    cp = links.copy(slab(far).at[0:half], buf.at[0, 0, 0:half], up)
    cm = links.copy(slab(far).at[half : 2 * half], buf.at[1, 0, half : 2 * half], down)
    yield

    def add(dst, part):
        dst[...] = (dst[...].astype(F32) + part[...].astype(F32)).astype(BF)

    for step in range(1, k):
        s = k - step
        dst = slab(wrap(i + s, n))
        cp.wait_recv()
        if step == 1:
            add(dst.at[0:half], buf.at[0, 0, 0:half])
        else:
            add(dst, buf.at[0, step - 1])
        cp = links.copy(dst, buf.at[0, step], up)
        dst = slab(wrap(i - s, n))
        cm.wait_recv()
        if step == 1:
            add(dst.at[half : 2 * half], buf.at[1, 0, half : 2 * half])
        else:
            add(dst, buf.at[1, step - 1])
        cm = links.copy(dst, buf.at[1, step], down)
        yield
    cp.wait_recv()
    cm.wait_recv()
    dst = slab(i)
    dst[...] = (
        dst[...].astype(F32) + buf[0, k - 1].astype(F32) + buf[1, k - 1].astype(F32)
    ).astype(BF)


def spread_reduce(links, n, i, slab, buf, devs):
    copies = [
        links.copy(slab(wrap(i + step, n)), buf.at[j], d)
        for j, (step, d) in enumerate(zip((1, n - 1, 2), devs))
    ]
    yield
    for c in copies:
        c.wait_recv()
    dst = slab(i)
    total = dst[...].astype(F32)
    for j in range(3):
        total += buf[j].astype(F32)
    dst[...] = total.astype(BF)


def contract(a, b, da, db):
    return lax.dot_general(a, b, (((da,), (db,)), ((), ())), preferred_element_type=F32)


def kernel(
    grad_out, queries, attended, keys, values, log_sums, seg, w_out, w_query, w_key, w_value,
    gin, dwo,
    tg, wv, qv, kvw, pb, raz, rax, rbx, rbz, ry,
    halo, ag, att_t, acc, qkv, kvg, kvback, kvland, ab, send, recv, loc,
):
    x = lax.axis_index("dp")
    r = lax.axis_index("context")
    t = lax.axis_index("tensor")
    yl, z = lax.div(r, NZ), lax.rem(r, NZ)
    yh, core = lax.div(t, 2), lax.rem(t, 2)
    y = 2 * yh + yl
    other = 1 - core
    partner = 2 * (1 - yh) + core

    def dev(x, y, z, core):
        return {
            "dp": x,
            "context": lax.rem(y, 2) * NZ + z,
            "tensor": lax.div(y, 2) * 2 + core,
        }

    xp, xm = dev(wrap(x + 1, NX), y, z, core), dev(wrap(x - 1, NX), y, z, core)
    yp, ym = dev(x, wrap(y + 1, NY), z, core), dev(x, wrap(y - 1, NY), z, core)
    zp, zm = dev(x, y, wrap(z + 1, NZ), core), dev(x, y, wrap(z - 1, NZ), core)
    pair = dev(x, 2 * yh + 1 - yl, z, core)
    sib = dev(x, y, z, other)
    far = dev(x, wrap(y + 2, NY), z, core)
    far_x = dev(wrap(x + 2, NX), y, z, core)
    far_sib = dev(x, wrap(y + 2, NY), z, other)
    n_ctx = 2 * NZ
    rp = {"dp": x, "context": wrap(r + 1, n_ctx), "tensor": t}
    rm = {"dp": x, "context": wrap(r - 1, n_ctx), "tensor": t}
    links = Links(send, recv)

    local = [
        pltpu.make_async_copy(w_out, wv.at[x, yl, z], loc.at[0]),
        pltpu.make_async_copy(w_query, qv.at[core, x, y, z], loc.at[1]),
        pltpu.make_async_copy(grad_out, tg.at[t], loc.at[2]),
        pltpu.make_async_copy(w_key, kvw.at[0:HD], loc.at[3]),
        pltpu.make_async_copy(w_value, kvw.at[HD : 2 * HD], loc.at[4]),
    ]
    for c in local:
        c.start()
    partners = (xp, xm, yp, ym, zp, zm, rp, rm, sib, far, far_sib, far_x)
    barrier = pltpu.get_barrier_semaphore()
    for d in partners:
        pl.semaphore_signal(barrier, inc=1, device_id=d, device_id_type=MESH)
    att_t[...] = attended[...].astype(F32).T.astype(BF)
    pl.semaphore_wait(barrier, len(partners))

    halo_copies = [
        links.copy(keys.at[0:SPAN], halo.at[0, 0], rp),
        links.copy(values.at[0:SPAN], halo.at[0, 1], rp),
        links.copy(keys.at[SPAN : 2 * SPAN], halo.at[1, 0], rm),
        links.copy(values.at[SPAN : 2 * SPAN], halo.at[1, 1], rm),
    ]
    chunk = NZ * HD
    n_chunks = 2 * NX
    far_copies, own_copy, sib_copies = [], [], []

    def cols(j):
        return pl.ds(((j % NX) * 2 + j // NX) * chunk, chunk)

    def send_far():
        j = len(far_copies)
        if j < n_chunks:
            far_copies.append(links.copy(grad_out.at[:, cols(j)], tg.at[t, :, cols(j)], far))

    def dw_chunk(j):
        if j == 0:
            local[2].wait()
            own_copy[0].wait_recv()
        sib_copies[j].wait_recv()
        xi, yi = j % NX, j // NX

        def step(q, carry):
            at = pl.ds(pl.multiple_of((xi * 2 + yi) * chunk + q * 4 * HD, 4 * HD), 4 * HD)
            lhs = tg[:, :, at].reshape(2 * SPAN, 4 * HD)
            part = jnp.dot(att_t[...], lhs, preferred_element_type=F32).astype(BF)
            for u in range(4):
                pb[xi, yi, 4 * q + u] = part[:, u * HD : (u + 1) * HD]
            return carry

        lax.fori_loop(0, 2, step, 0)

    def grads_stream(first):
        yield
        if first == 0:
            for _ in range(WINDOW):
                send_far()
            own_copy.append(links.copy(grad_out, tg.at[t], sib))
        for j in range(first, first + NX):
            yield
            far_copies[j].wait_recv()
            send_far()
            got = tg.at[partner, :, cols(j)]
            sib_copies.append(links.copy(got, got, sib))
            if j > first:
                yield
                dw_chunk(j - 1)
        yield
        dw_chunk(first + NX - 1)

    def w_out_stream(part):
        hs = pl.ds(0, W_ROWS) if part == 0 else pl.ds(W_ROWS, HD - W_ROWS)
        yield
        c = links.copy(wv.at[x, yl, z, hs], wv.at[x, yl, z, hs], pair)
        yield
        c.wait_recv()
        if part == 0:
            yield from spread(links, wv.at[x, :, z, hs], (xp, xm, far_x))
            yield from ring_gather(links, NZ, z, lambda i: wv.at[:, :, i, hs], 2, zp, zm)
        else:
            yield from ring_gather(links, NZ, z, lambda i: wv.at[x, :, i, hs], 1, zp, zm)
            yield from ring_gather(links, NX, x, lambda i: wv.at[i, :, :, hs], 1, xp, xm)

    q_waits = []

    def w_query_stream(part):
        lo_row, n_rows = Q_ROWS[part]
        hs = pl.ds(lo_row, n_rows)

        def hand_over(piece):
            q_waits.append(links.copy(piece, piece, sib))

        yield
        if part == 2:
            yield from ring_gather(links, NZ, z, lambda i: qv.at[core, x, y, i, hs], None, zp, zm)
            yield from ring_gather(links, NX, x, lambda i: qv.at[core, i, y, :, hs], 4, xp, xm)
            yield
            yield from ring_gather(
                links, NY, y, lambda i: qv.at[core, :, i, :, hs], 2, yp, ym, hand_over
            )
            return
        yield from spread(links, qv.at[core, x, y, z, hs], (yp, ym, far))
        if part == 0:
            yield from spread(links, qv.at[core, x, :, z, hs], (xp, xm, far_x))
            yield
            yield from ring_gather(
                links, NZ, z, lambda i: qv.at[core, :, :, i, hs], 2, zp, zm, hand_over
            )
        else:
            yield from ring_gather(links, NZ, z, lambda i: qv.at[core, x, :, i, hs], 2, zp, zm)
            yield
            yield from ring_gather(
                links, NX, x, lambda i: qv.at[core, i, :, :, hs], 2, xp, xm, hand_over
            )

    lo, hi = pl.ds(0, HD), pl.ds(HD, HD)

    def reduce_a(yi):
        yield
        yield from ring_reduce(
            links, NZ, z, lambda i: pb.at[:, yi, i, lo], raz.at[yi], 2, zp, zm
        )
        yield from spread_reduce(
            links, NX, x, lambda i: pb.at[i, yi, z, lo], rax.at[yi], (xp, xm, far_x)
        )

    def reduce_b(yi):
        yield
        yield from ring_reduce(
            links, NX, x, lambda i: pb.at[i, yi, :, hi], rbx.at[yi], 4, xp, xm
        )
        yield from ring_reduce(
            links, NZ, z, lambda i: pb.at[x, yi, i, hi], rbz.at[yi], 64, zp, zm
        )

    def pair_sum():
        yield
        c = links.copy(pb.at[x, 1 - yl, z], ry, pair)
        yield
        c.wait_recv()
        dwo[...] = (pb[x, yl, z].astype(F32) + ry[...].astype(F32)).T

    def ag_steps(first):
        def step(j, carry):
            at = pl.ds(pl.multiple_of(j * 4 * HD, 4 * HD), 4 * HD)
            lhs = tg[:, :, at].reshape(2 * SPAN, 4 * HD)
            xi, rest = lax.div(j, 4), lax.rem(j, 4)
            yi, zi = lax.div(rest, 2), lax.rem(rest, 2) * 4
            rhs = wv[xi, yi, pl.ds(zi, 4)].reshape(4 * HD, 2 * HD)
            acc[...] += jnp.dot(lhs, rhs, preferred_element_type=F32)
            return carry

        lax.fori_loop(first, first + 4, step, 0)

    last = r == n_ctx - 1
    inv_root = 1.0 / math.sqrt(HD)
    row_at = lax.broadcasted_iota(jnp.int32, (SPAN, SPAN), 0)
    col_at = lax.broadcasted_iota(jnp.int32, (SPAN, SPAN), 1)
    eye = row_at == col_at
    q_at = lax.broadcasted_iota(jnp.int32, (SPAN, 2 * SPAN), 0)
    k_at = lax.broadcasted_iota(jnp.int32, (SPAN, 2 * SPAN), 1) - SPAN

    def column(row, zero):
        return jnp.sum(jnp.where(eye, row, zero), axis=1, keepdims=True)

    def seg_of(span):
        return seg[:, pl.ds(pl.multiple_of(span * SPAN, SPAN), SPAN)]

    def unit(b, h):
        rows_b, cols_h = pl.ds(b * SPAN, SPAN), pl.ds(h * HD, HD)
        span = r if b == 0 else 2 * n_ctx - 1 - r
        seg_q = seg_of(span)
        seg_k = jnp.concatenate([seg_of(jnp.maximum(span - 1, 0)), seg_q], axis=1)
        allowed = (
            (k_at <= q_at)
            & (k_at + span * SPAN >= 0)
            & (seg_k == column(seg_q, 0))
        )
        prev_k, prev_v = halo[b, 0], halo[b, 1]
        if b == 1:
            prev_k = jnp.where(last, keys[0:SPAN], prev_k)
            prev_v = jnp.where(last, values[0:SPAN], prev_v)
        k_cat = jnp.concatenate([prev_k, keys[rows_b]], axis=0)
        v_cat = jnp.concatenate([prev_v, values[rows_b]], axis=0)
        qb, db = queries[rows_b, cols_h], ag[rows_b, cols_h]
        delta = jnp.sum(
            db.astype(F32) * attended[rows_b, cols_h].astype(F32), axis=1, keepdims=True
        )
        lse = column(log_sums[h : h + 1, rows_b], 0.0)
        scores = contract(qb, k_cat, 1, 1) * inv_root
        prob = jnp.where(allowed, jnp.exp(scores - lse), 0.0)
        dprob = contract(db, v_cat, 1, 1)
        dscore = (prob * (dprob - delta)).astype(BF)
        dq = jnp.dot(dscore, k_cat, preferred_element_type=F32) * inv_root
        qkv[rows_b, cols_h] = dq.astype(BF)
        kg = contract(dscore, qb, 0, 0) * inv_root
        vg = contract(prob.astype(BF), db, 0, 0)
        if h == 0:
            kvg[b, :, 0:HD] = kg
            kvg[b, :, HD : 2 * HD] = vg
        else:
            kvg[b, :, 0:HD] += kg
            kvg[b, :, HD : 2 * HD] += vg

    def rows_of(d):
        return pl.ds(pl.multiple_of(d * HD, HD), HD)

    def attention_stream():
        for part in range(4):
            yield
            if part == 0:
                acc[...] = jnp.zeros_like(acc)
            ag_steps(4 * part)
        yield
        ag[...] = acc[...].astype(BF)
        for c in halo_copies:
            c.wait_recv()
        for b in range(2):
            for h in range(2):
                unit(b, h)
        kvback[0] = kvg[0, 0:SPAN].astype(BF)
        kvback[1] = jnp.where(last, 0.0, kvg[1, 0:SPAN]).astype(BF)
        to_left = links.copy(kvback.at[0], kvland.at[0], rm)
        to_right = links.copy(kvback.at[1], kvland.at[1], rp)
        yield
        to_left.wait_recv()
        to_right.wait_recv()
        low = (
            kvg[0, SPAN : 2 * SPAN]
            + jnp.where(last, kvg[1, 0:SPAN], 0.0)
            + kvland[0].astype(F32)
        )
        high = kvg[1, SPAN : 2 * SPAN] + kvland[1].astype(F32)
        qkv[0:SPAN, 2 * HD : 4 * HD] = low.astype(BF)
        qkv[SPAN : 2 * SPAN, 2 * HD : 4 * HD] = high.astype(BF)
        swaps = [
            links.copy(qkv.at[rows_of(partner)], ab.at[t], far),
            links.copy(qkv.at[rows_of(2 * (1 - yh) + other)], ab.at[t], far_sib),
            links.copy(qkv.at[rows_of(2 * yh + other)], ab.at[t], sib),
        ]
        ab[t] = qkv[rows_of(t)]
        yield
        for c in swaps:
            c.wait_recv()

    def out_stream():
        yield
        local[3].wait()
        local[4].wait()
        for c in q_waits:
            c.wait_recv()
        kv_sum = jnp.sum(ab[:, :, 2 * HD : 4 * HD].astype(F32), axis=0).astype(BF)

        def step(j, carry):
            xi, yi = lax.div(j, 2), lax.rem(j, 2)
            for q in range(4):
                at = pl.ds(pl.multiple_of(j * chunk + q * 2 * HD, 2 * HD), 2 * HD)
                total = jnp.dot(kv_sum, kvw[:, at], preferred_element_type=F32)
                for g in range(4):
                    heads = qv.at[g % 2, xi, 2 * (g // 2) + yi]
                    rhs = jnp.concatenate([heads[2 * q], heads[2 * q + 1]], axis=1)
                    total += jnp.dot(ab[g, :, 0 : 2 * HD], rhs, preferred_element_type=F32)
                gin[:, at] = total.astype(BF)
            return carry

        for part in range(4):
            lax.fori_loop(2 * part, 2 * part + 2, step, 0)
            if part < 3:
                yield

    local[0].wait()
    local[1].wait()
    live = {
        "w": w_out_stream(0),
        "v": w_out_stream(1),
        "g": grads_stream(0),
        "h": grads_stream(NX),
        "q": w_query_stream(0),
        "r": w_query_stream(1),
        "s": w_query_stream(2),
        "a": reduce_a(0),
        "b": reduce_b(0),
        "c": reduce_a(1),
        "d": reduce_b(1),
        "y": pair_sum(),
        "t": attention_stream(),
        "p": out_stream(),
    }
    for stream in live.values():
        next(stream)
    for name in "".join(ORDER):
        next(live[name], 0)
    for stream in live.values():
        assert next(stream, 0) == 0
    for c in links.started:
        c.wait_send()


def on_device(
    grad_out, queries, attended, keys, values, log_sums, segment_ids, w_out, w_query, w_key, w_value
):
    vmem = pl.BlockSpec(memory_space=pltpu.VMEM)
    hbm = pl.BlockSpec(memory_space=pl.ANY)
    own, model = grad_out.shape
    blocks = (NX, 2, NZ)
    return pl.pallas_call(
        kernel,
        out_shape=(
            jax.ShapeDtypeStruct((own, model), BF),
            jax.ShapeDtypeStruct((HD, 2 * HD), F32),
        ),
        in_specs=[hbm] + [vmem] * 6 + [hbm] * 4,
        out_specs=(vmem, vmem),
        scratch_shapes=[
            pltpu.VMEM((4, own, model), BF),
            pltpu.VMEM(blocks + (HD, 2 * HD), BF),
            pltpu.VMEM((2, NX, NY, NZ, 2 * HD, HD), BF),
            pltpu.VMEM((2 * HD, model), BF),
            pltpu.VMEM(blocks + (2 * HD, HD), BF),
            pltpu.VMEM((2, 2, 4, NX, HD, HD), BF),
            pltpu.VMEM((2, 3, HD, HD), BF),
            pltpu.VMEM((2, 2, 2, NZ, HD, HD), BF),
            pltpu.VMEM((2, 2, 4, HD, HD), BF),
            pltpu.VMEM((2 * HD, HD), BF),
            pltpu.VMEM((2, 2, SPAN, HD), BF),
            pltpu.VMEM((2 * SPAN, 2 * HD), BF),
            pltpu.VMEM((2 * HD, 2 * SPAN), BF),
            pltpu.VMEM((2 * SPAN, 2 * HD), F32),
            pltpu.VMEM((2 * SPAN, 4 * HD), BF),
            pltpu.VMEM((2, 2 * SPAN, 2 * HD), F32),
            pltpu.VMEM((2, SPAN, 2 * HD), BF),
            pltpu.VMEM((2, SPAN, 2 * HD), BF),
            pltpu.VMEM((4, HD, 4 * HD), BF),
            pltpu.SemaphoreType.DMA((N_REMOTE,)),
            pltpu.SemaphoreType.DMA((N_REMOTE,)),
            pltpu.SemaphoreType.DMA((N_LOCAL,)),
        ],
        compiler_params=pltpu.CompilerParams(
            collective_id=0, has_side_effects=True, vmem_limit_bytes=60 * 2**20
        ),
    )(
        grad_out, queries, attended, keys, values, log_sums, segment_ids, w_out, w_query, w_key, w_value
    )


def solution(mesh):
    placed = (
        P(("dp", "context", "tensor"), None),
        P(("dp", "context"), "tensor"),
        P(("dp", "context"), "tensor"),
        P(("dp", "context"), None),
        P(("dp", "context"), None),
        P("tensor", ("dp", "context")),
        P("dp", None),
        P(("dp", "context"), "tensor"),
        P("tensor", ("dp", "context")),
        P(),
        P(),
    )
    return jax.shard_map(
        on_device,
        mesh=mesh,
        in_specs=placed,
        out_specs=(P(("dp", "context", "tensor"), None), P(("dp", "context"), "tensor")),
        check_vma=False,
    )
```

```python
import functools
import math

import jax
import jax.numpy as jnp
from jax import lax
from jax.experimental import pallas as pl
from jax.experimental.pallas import tpu as pltpu
from jax.sharding import PartitionSpec as P

MESH = pl.DeviceIdType.MESH
BF = jnp.bfloat16
F32 = jnp.float32
NX, NY, NZ = 4, 4, 8
SPAN = 256
HD = 128
N_REMOTE = 256
N_LOCAL = 16
WINDOW = 8
W_ROWS = 64
Q_ROWS = ((0, 64), (64, 96), (160, 96))
ORDER = (
    "swvrqwgvsrvqswvsrqqsgrggwgggVvqVsggbvVwR",
    "hhhqbVshhrswRVhhbahhcdbwqrcRaVbtdtRcttas",
    "tRqdaRtdcdbsacdtabpcdypppy",
)


def wrap(i, n):
    return lax.rem(i + n, n)


class Links:
    def __init__(self, send, recv):
        self.send, self.recv, self.started = send, recv, []

    def copy(self, src, dst, dev):
        n = len(self.started)
        c = pltpu.make_async_remote_copy(
            src_ref=src,
            dst_ref=dst,
            send_sem=self.send.at[n],
            recv_sem=self.recv.at[n],
            device_id=dev,
            device_id_type=MESH,
        )
        c.start()
        self.started.append(c)
        return c


def ring_gather(links, n, i, slab, half, up, down, arrived=None):
    k = n // 2
    cp = links.copy(slab(i), slab(i), up)
    cm = links.copy(slab(i), slab(i), down)
    if arrived is not None:
        arrived(slab(i))
    for s in range(1, k):
        yield
        before, after = slab(wrap(i - s, n)), slab(wrap(i + s, n))
        cp.wait_recv()
        piece = before if s < k - 1 or half is None else before.at[0:half]
        cp = links.copy(piece, piece, up)
        if arrived is not None:
            arrived(before)
        cm.wait_recv()
        if s < k - 1:
            cm = links.copy(after, after, down)
        elif half is not None:
            piece = after.at[half : 2 * half]
            cm = links.copy(piece, piece, down)
        else:
            cm = None
        if arrived is not None:
            arrived(after)
    yield
    cp.wait_recv()
    if cm is not None:
        cm.wait_recv()
    if arrived is not None:
        arrived(slab(wrap(i + k, n)))


def pipelined_gather(links, z, x, slab, half, z_devs, x_devs):
    zk = NZ // 2
    sent = []

    def along_x(zs):
        ups, downs = [], []
        for zi in zs:
            piece = slab(x, zi)
            ups.append(links.copy(piece, piece, x_devs[0]))
            downs.append(links.copy(piece, piece, x_devs[1]))
        sent.append((zs, ups, downs))

    def first():
        own = slab(x, z)
        cp, cm = links.copy(own, own, z_devs[0]), links.copy(own, own, z_devs[1])
        along_x((z,))
        for s in range(1, zk):
            yield
            before, after = wrap(z - s, NZ), wrap(z + s, NZ)
            cp.wait_recv()
            cm.wait_recv()
            up, down = slab(x, before), slab(x, after)
            if s == zk - 1:
                up, down = up.at[0:half], down.at[half : 2 * half]
            cp, cm = links.copy(up, up, z_devs[0]), links.copy(down, down, z_devs[1])
            along_x((before, after))
        yield
        cp.wait_recv()
        cm.wait_recv()
        along_x((wrap(z + zk, NZ),))

    def second():
        before, after = wrap(x - 1, NX), wrap(x + 1, NX)
        halves = []
        for k in range(zk + 1):
            yield
            zs, ups, downs = sent[k]
            for zi, up, down in zip(zs, ups, downs):
                up.wait_recv()
                down.wait_recv()
                got = slab(before, zi)
                piece = got.at[0:half]
                halves.append(links.copy(piece, piece, x_devs[0]))
                got = slab(after, zi)
                piece = got.at[half : 2 * half]
                halves.append(links.copy(piece, piece, x_devs[1]))
        yield
        for c in halves:
            c.wait_recv()

    return first, second


def spread(links, piece, devs, source=None):
    source = piece if source is None else source
    copies = [links.copy(source, piece, d) for d in devs]
    yield
    for c in copies:
        c.wait_recv()


def ring_reduce(links, n, i, slab, buf, half, up, down):
    k = n // 2
    far = wrap(i + k, n)
    cp = links.copy(slab(far).at[0:half], buf.at[0, 0, 0:half], up)
    cm = links.copy(slab(far).at[half : 2 * half], buf.at[1, 0, half : 2 * half], down)
    yield

    def add(dst, part):
        dst[...] = (dst[...].astype(F32) + part[...].astype(F32)).astype(BF)

    for step in range(1, k):
        s = k - step
        dst = slab(wrap(i + s, n))
        cp.wait_recv()
        if step == 1:
            add(dst.at[0:half], buf.at[0, 0, 0:half])
        else:
            add(dst, buf.at[0, step - 1])
        cp = links.copy(dst, buf.at[0, step], up)
        dst = slab(wrap(i - s, n))
        cm.wait_recv()
        if step == 1:
            add(dst.at[half : 2 * half], buf.at[1, 0, half : 2 * half])
        else:
            add(dst, buf.at[1, step - 1])
        cm = links.copy(dst, buf.at[1, step], down)
        yield
    cp.wait_recv()
    cm.wait_recv()
    dst = slab(i)
    dst[...] = (
        dst[...].astype(F32) + buf[0, k - 1].astype(F32) + buf[1, k - 1].astype(F32)
    ).astype(BF)


def spread_reduce(links, n, i, slab, buf, devs):
    copies = [
        links.copy(slab(wrap(i + step, n)), buf.at[j], d)
        for j, (step, d) in enumerate(zip((1, n - 1, 2), devs))
    ]
    yield
    for c in copies:
        c.wait_recv()
    dst = slab(i)
    total = dst[...].astype(F32)
    for j in range(3):
        total += buf[j].astype(F32)
    dst[...] = total.astype(BF)


def contract(a, b, da, db):
    return lax.dot_general(a, b, (((da,), (db,)), ((), ())), preferred_element_type=F32)


def kernel(
    grad_out, queries_in, attended_in, keys_in, values_in, log_sums_in, seg_in,
    w_out, w_query, w_key, w_value,
    gin_out, dwo,
    queries, attended, keys, values, log_sums, seg, gin, tg, wv, qv, kvw, pb, raz, rax, rbx, rbz, ry,
    halo, ag, att_t, acc, qkv, kvg, kvback, kvland, ab, send, recv, loc,
):
    x = lax.axis_index("dp")
    r = lax.axis_index("context")
    t = lax.axis_index("tensor")
    yl, z = lax.div(r, NZ), lax.rem(r, NZ)
    yh, core = lax.div(t, 2), lax.rem(t, 2)
    y = 2 * yh + yl
    other = 1 - core
    partner = 2 * (1 - yh) + core

    def dev(x, y, z, core):
        return {
            "dp": x,
            "context": lax.rem(y, 2) * NZ + z,
            "tensor": lax.div(y, 2) * 2 + core,
        }

    xp, xm = dev(wrap(x + 1, NX), y, z, core), dev(wrap(x - 1, NX), y, z, core)
    yp, ym = dev(x, wrap(y + 1, NY), z, core), dev(x, wrap(y - 1, NY), z, core)
    zp, zm = dev(x, y, wrap(z + 1, NZ), core), dev(x, y, wrap(z - 1, NZ), core)
    pair = dev(x, 2 * yh + 1 - yl, z, core)
    sib = dev(x, y, z, other)
    far = dev(x, wrap(y + 2, NY), z, core)
    far_x = dev(wrap(x + 2, NX), y, z, core)
    far_sib = dev(x, wrap(y + 2, NY), z, other)
    n_ctx = 2 * NZ
    rp = {"dp": x, "context": wrap(r + 1, n_ctx), "tensor": t}
    rm = {"dp": x, "context": wrap(r - 1, n_ctx), "tensor": t}
    links = Links(send, recv)

    local = [
        pltpu.make_async_copy(w_out, wv.at[x, yl, z], loc.at[0]),
        pltpu.make_async_copy(w_query, qv.at[core, x, y, z], loc.at[1]),
        pltpu.make_async_copy(grad_out, tg.at[t], loc.at[2]),
        pltpu.make_async_copy(w_key, kvw.at[0:HD], loc.at[3]),
        pltpu.make_async_copy(w_value, kvw.at[HD : 2 * HD], loc.at[4]),
        pltpu.make_async_copy(attended_in, attended, loc.at[5]),
        pltpu.make_async_copy(queries_in, queries, loc.at[6]),
        pltpu.make_async_copy(keys_in, keys, loc.at[7]),
        pltpu.make_async_copy(values_in, values, loc.at[8]),
        pltpu.make_async_copy(log_sums_in, log_sums, loc.at[9]),
        pltpu.make_async_copy(seg_in, seg, loc.at[10]),
    ]
    partners = (xp, xm, yp, ym, zp, zm, rp, rm, sib, far, far_sib, far_x)
    barrier = pltpu.get_barrier_semaphore()
    for d in partners:
        pl.semaphore_signal(barrier, inc=1, device_id=d, device_id_type=MESH)
    for c in local:
        c.start()
    pl.semaphore_wait(barrier, len(partners))

    chunk = NZ * HD
    n_chunks = 2 * NX
    ready = set()
    far_copies, own_copy, sib_copies, halo_copies = [], [], [], []

    def cols(j):
        return pl.ds(((j % NX) * 2 + j // NX) * chunk, chunk)

    def send_far():
        j = len(far_copies)
        if j < n_chunks:
            far_copies.append(links.copy(grad_out.at[:, cols(j)], tg.at[t, :, cols(j)], far))

    def dw_chunk(j):
        if j == 0:
            local[2].wait()
            own_copy[0].wait_recv()
        sib_copies[j].wait_recv()
        xi, yi = j % NX, j // NX

        def step(q, carry):
            at = pl.ds(pl.multiple_of((xi * 2 + yi) * chunk + q * 4 * HD, 4 * HD), 4 * HD)
            lhs = tg[:, :, at].reshape(2 * SPAN, 4 * HD)
            part = jnp.dot(att_t[...], lhs, preferred_element_type=F32).astype(BF)
            for u in range(4):
                pb[xi, yi, 4 * q + u] = part[:, u * HD : (u + 1) * HD]
            return carry

        lax.fori_loop(0, 2, step, 0)

    def grads_stream(first):
        yield
        if first == 0:
            for _ in range(WINDOW):
                send_far()
            own_copy.append(links.copy(grad_out, tg.at[t], sib))
        for j in range(first, first + NX):
            yield
            far_copies[j].wait_recv()
            send_far()
            got = tg.at[partner, :, cols(j)]
            sib_copies.append(links.copy(got, got, sib))
            if j > first:
                yield
                dw_chunk(j - 1)
        yield
        dw_chunk(first + NX - 1)

    def w_out_stream(part):
        hs = pl.ds(0, W_ROWS) if part == 0 else pl.ds(W_ROWS, HD - W_ROWS)
        yield
        c = links.copy(w_out.at[hs], wv.at[x, yl, z, hs], pair)
        yield
        if 0 not in ready:
            local[0].wait()
            ready.add(0)
        c.wait_recv()
        if part == 0:
            yield from spread(links, wv.at[x, :, z, hs], (xp, xm, far_x))
            yield from ring_gather(links, NZ, z, lambda i: wv.at[:, :, i, hs], 2, zp, zm)
        else:
            yield from w_first()

    w_rest = pl.ds(W_ROWS, HD - W_ROWS)
    w_first, w_second = pipelined_gather(
        links, z, x, lambda i, j: wv.at[i, :, j, w_rest], 1, (zp, zm), (xp, xm)
    )
    q_waits = []

    def w_query_stream(part):
        lo_row, n_rows = Q_ROWS[part]
        hs = pl.ds(lo_row, n_rows)

        def hand_over(piece):
            q_waits.append(links.copy(piece, piece, sib))

        yield
        if part == 2:
            if 1 not in ready:
                local[1].wait()
                ready.add(1)
            yield from ring_gather(links, NZ, z, lambda i: qv.at[core, x, y, i, hs], None, zp, zm)
            yield from ring_gather(links, NX, x, lambda i: qv.at[core, i, y, :, hs], 4, xp, xm)
            yield
            yield from ring_gather(
                links, NY, y, lambda i: qv.at[core, :, i, :, hs], 2, yp, ym, hand_over
            )
            return
        yield from spread(links, qv.at[core, x, y, z, hs], (yp, ym, far), w_query.at[hs])
        if 1 not in ready:
            local[1].wait()
            ready.add(1)
        if part == 0:
            yield from spread(links, qv.at[core, x, :, z, hs], (xp, xm, far_x))
            yield
            yield from ring_gather(
                links, NZ, z, lambda i: qv.at[core, :, :, i, hs], 2, zp, zm, hand_over
            )
        else:
            yield from q_first()

    q_rest = pl.ds(Q_ROWS[1][0], Q_ROWS[1][1])
    q_first, q_second = pipelined_gather(
        links, z, x, lambda i, j: qv.at[core, i, :, j, q_rest], 2, (zp, zm), (xp, xm)
    )

    def q_tail():
        yield from q_second()
        for i in range(NX):
            piece = qv.at[core, i, :, :, q_rest]
            q_waits.append(links.copy(piece, piece, sib))

    lo, hi = pl.ds(0, HD), pl.ds(HD, HD)

    def reduce_a(yi):
        yield
        yield from ring_reduce(
            links, NZ, z, lambda i: pb.at[:, yi, i, lo], raz.at[yi], 2, zp, zm
        )
        yield from spread_reduce(
            links, NX, x, lambda i: pb.at[i, yi, z, lo], rax.at[yi], (xp, xm, far_x)
        )

    def reduce_b(yi):
        yield
        yield from ring_reduce(
            links, NX, x, lambda i: pb.at[i, yi, :, hi], rbx.at[yi], 4, xp, xm
        )
        yield from ring_reduce(
            links, NZ, z, lambda i: pb.at[x, yi, i, hi], rbz.at[yi], 64, zp, zm
        )

    def pair_sum():
        yield
        c = links.copy(pb.at[x, 1 - yl, z], ry, pair)
        yield
        c.wait_recv()
        dwo[...] = (pb[x, yl, z].astype(F32) + ry[...].astype(F32)).T

    def ag_steps(first):
        def step(j, carry):
            at = pl.ds(pl.multiple_of(j * 4 * HD, 4 * HD), 4 * HD)
            lhs = tg[:, :, at].reshape(2 * SPAN, 4 * HD)
            xi, rest = lax.div(j, 4), lax.rem(j, 4)
            yi, zi = lax.div(rest, 2), lax.rem(rest, 2) * 4
            rhs = wv[xi, yi, pl.ds(zi, 4)].reshape(4 * HD, 2 * HD)
            acc[...] += jnp.dot(lhs, rhs, preferred_element_type=F32)
            return carry

        lax.fori_loop(first, first + 4, step, 0)

    last = r == n_ctx - 1
    inv_root = 1.0 / math.sqrt(HD)
    row_at = lax.broadcasted_iota(jnp.int32, (SPAN, SPAN), 0)
    col_at = lax.broadcasted_iota(jnp.int32, (SPAN, SPAN), 1)
    eye = row_at == col_at
    q_at = lax.broadcasted_iota(jnp.int32, (SPAN, 2 * SPAN), 0)
    k_at = lax.broadcasted_iota(jnp.int32, (SPAN, 2 * SPAN), 1) - SPAN

    def column(row, zero):
        return jnp.sum(jnp.where(eye, row, zero), axis=1, keepdims=True)

    def seg_of(span):
        return seg[:, pl.ds(pl.multiple_of(span * SPAN, SPAN), SPAN)]

    def unit(b, h):
        rows_b, cols_h = pl.ds(b * SPAN, SPAN), pl.ds(h * HD, HD)
        span = r if b == 0 else 2 * n_ctx - 1 - r
        seg_q = seg_of(span)
        seg_k = jnp.concatenate([seg_of(jnp.maximum(span - 1, 0)), seg_q], axis=1)
        allowed = (
            (k_at <= q_at)
            & (k_at + span * SPAN >= 0)
            & (seg_k == column(seg_q, 0))
        )
        prev_k, prev_v = halo[b, 0], halo[b, 1]
        if b == 1:
            prev_k = jnp.where(last, keys[0:SPAN], prev_k)
            prev_v = jnp.where(last, values[0:SPAN], prev_v)
        k_cat = jnp.concatenate([prev_k, keys[rows_b]], axis=0)
        v_cat = jnp.concatenate([prev_v, values[rows_b]], axis=0)
        qb, db = queries[rows_b, cols_h], ag[rows_b, cols_h]
        delta = jnp.sum(
            db.astype(F32) * attended[rows_b, cols_h].astype(F32), axis=1, keepdims=True
        )
        lse = column(log_sums[h : h + 1, rows_b], 0.0)
        scores = contract(qb, k_cat, 1, 1) * inv_root
        prob = jnp.where(allowed, jnp.exp(scores - lse), 0.0)
        dprob = contract(db, v_cat, 1, 1)
        dscore = (prob * (dprob - delta)).astype(BF)
        dq = jnp.dot(dscore, k_cat, preferred_element_type=F32) * inv_root
        qkv[rows_b, cols_h] = dq.astype(BF)
        kg = contract(dscore, qb, 0, 0) * inv_root
        vg = contract(prob.astype(BF), db, 0, 0)
        if h == 0:
            kvg[b, :, 0:HD] = kg
            kvg[b, :, HD : 2 * HD] = vg
        else:
            kvg[b, :, 0:HD] += kg
            kvg[b, :, HD : 2 * HD] += vg

    def rows_of(d):
        return pl.ds(pl.multiple_of(d * HD, HD), HD)

    def attention_stream():
        for part in range(4):
            yield
            if part == 0:
                acc[...] = jnp.zeros_like(acc)
            ag_steps(4 * part)
        yield
        ag[...] = acc[...].astype(BF)
        for c in local[6:]:
            c.wait()
        for c in halo_copies:
            c.wait_recv()
        for b in range(2):
            for h in range(2):
                unit(b, h)
        kvback[0] = kvg[0, 0:SPAN].astype(BF)
        kvback[1] = jnp.where(last, 0.0, kvg[1, 0:SPAN]).astype(BF)
        to_left = links.copy(kvback.at[0], kvland.at[0], rm)
        to_right = links.copy(kvback.at[1], kvland.at[1], rp)
        yield
        to_left.wait_recv()
        to_right.wait_recv()
        low = (
            kvg[0, SPAN : 2 * SPAN]
            + jnp.where(last, kvg[1, 0:SPAN], 0.0)
            + kvland[0].astype(F32)
        )
        high = kvg[1, SPAN : 2 * SPAN] + kvland[1].astype(F32)
        qkv[0:SPAN, 2 * HD : 4 * HD] = low.astype(BF)
        qkv[SPAN : 2 * SPAN, 2 * HD : 4 * HD] = high.astype(BF)
        swaps = [
            links.copy(qkv.at[rows_of(partner)], ab.at[t], far),
            links.copy(qkv.at[rows_of(2 * (1 - yh) + other)], ab.at[t], far_sib),
            links.copy(qkv.at[rows_of(2 * yh + other)], ab.at[t], sib),
        ]
        ab[t] = qkv[rows_of(t)]
        yield
        for c in swaps:
            c.wait_recv()

    out_copies = []

    def out_stream():
        yield
        local[3].wait()
        local[4].wait()
        for c in q_waits:
            c.wait_recv()
        kv_sum = jnp.sum(ab[:, :, 2 * HD : 4 * HD].astype(F32), axis=0).astype(BF)

        def step(j, carry):
            xi, yi = lax.div(j, 2), lax.rem(j, 2)
            for q in range(4):
                at = pl.ds(pl.multiple_of(j * chunk + q * 2 * HD, 2 * HD), 2 * HD)
                total = jnp.dot(kv_sum, kvw[:, at], preferred_element_type=F32)
                for g in range(4):
                    heads = qv.at[g % 2, xi, 2 * (g // 2) + yi]
                    rhs = jnp.concatenate([heads[2 * q], heads[2 * q + 1]], axis=1)
                    total += jnp.dot(ab[g, :, 0 : 2 * HD], rhs, preferred_element_type=F32)
                gin[:, at] = total.astype(BF)
            return carry

        for part in range(4):
            lax.fori_loop(2 * part, 2 * part + 2, step, 0)
            at = pl.ds(2 * part * chunk, 2 * chunk)
            out_copies.append(pltpu.make_async_copy(gin.at[:, at], gin_out.at[:, at], loc.at[11 + part]))
            out_copies[-1].start()
            if part < 3:
                yield

    live = {
        "w": w_out_stream(0),
        "v": w_out_stream(1),
        "g": grads_stream(0),
        "h": grads_stream(NX),
        "q": w_query_stream(0),
        "r": w_query_stream(1),
        "s": w_query_stream(2),
        "a": reduce_a(0),
        "b": reduce_b(0),
        "c": reduce_a(1),
        "d": reduce_b(1),
        "y": pair_sum(),
        "t": attention_stream(),
        "p": out_stream(),
        "V": w_second(),
        "R": q_tail(),
    }
    for stream in live.values():
        next(stream)
    for n, name in enumerate("".join(ORDER)):
        next(live[name], 0)
        if n == 5:
            halo_copies.extend([
                links.copy(keys_in.at[0:SPAN], halo.at[0, 0], rp),
                links.copy(values_in.at[0:SPAN], halo.at[0, 1], rp),
                links.copy(keys_in.at[SPAN : 2 * SPAN], halo.at[1, 0], rm),
                links.copy(values_in.at[SPAN : 2 * SPAN], halo.at[1, 1], rm),
            ])
            local[5].wait()
            att_t[...] = attended[...].astype(F32).T.astype(BF)
    for stream in live.values():
        assert next(stream, 0) == 0
    for c in links.started:
        c.wait_send()
    for c in out_copies:
        c.wait()


def on_device(
    grad_out, queries, attended, keys, values, log_sums, segment_ids, w_out, w_query, w_key, w_value
):
    vmem = pl.BlockSpec(memory_space=pltpu.VMEM)
    hbm = pl.BlockSpec(memory_space=pl.ANY)
    own, model = grad_out.shape
    blocks = (NX, 2, NZ)
    return pl.pallas_call(
        kernel,
        out_shape=(
            jax.ShapeDtypeStruct((own, model), BF),
            jax.ShapeDtypeStruct((HD, 2 * HD), F32),
        ),
        in_specs=[hbm] * 11,
        out_specs=(hbm, vmem),
        scratch_shapes=[
            pltpu.VMEM(queries.shape, BF),
            pltpu.VMEM(attended.shape, BF),
            pltpu.VMEM(keys.shape, BF),
            pltpu.VMEM(values.shape, BF),
            pltpu.VMEM(log_sums.shape, F32),
            pltpu.VMEM(segment_ids.shape, jnp.int32),
            pltpu.VMEM((own, model), BF),
            pltpu.VMEM((4, own, model), BF),
            pltpu.VMEM(blocks + (HD, 2 * HD), BF),
            pltpu.VMEM((2, NX, NY, NZ, 2 * HD, HD), BF),
            pltpu.VMEM((2 * HD, model), BF),
            pltpu.VMEM(blocks + (2 * HD, HD), BF),
            pltpu.VMEM((2, 2, 4, NX, HD, HD), BF),
            pltpu.VMEM((2, 3, HD, HD), BF),
            pltpu.VMEM((2, 2, 2, NZ, HD, HD), BF),
            pltpu.VMEM((2, 2, 4, HD, HD), BF),
            pltpu.VMEM((2 * HD, HD), BF),
            pltpu.VMEM((2, 2, SPAN, HD), BF),
            pltpu.VMEM((2 * SPAN, 2 * HD), BF),
            pltpu.VMEM((2 * HD, 2 * SPAN), BF),
            pltpu.VMEM((2 * SPAN, 2 * HD), F32),
            pltpu.VMEM((2 * SPAN, 4 * HD), BF),
            pltpu.VMEM((2, 2 * SPAN, 2 * HD), F32),
            pltpu.VMEM((2, SPAN, 2 * HD), BF),
            pltpu.VMEM((2, SPAN, 2 * HD), BF),
            pltpu.VMEM((4, HD, 4 * HD), BF),
            pltpu.SemaphoreType.DMA((N_REMOTE,)),
            pltpu.SemaphoreType.DMA((N_REMOTE,)),
            pltpu.SemaphoreType.DMA((N_LOCAL,)),
        ],
        compiler_params=pltpu.CompilerParams(
            collective_id=0, has_side_effects=True, vmem_limit_bytes=60 * 2**20
        ),
    )(
        grad_out, queries, attended, keys, values, log_sums, segment_ids, w_out, w_query, w_key, w_value
    )


def solution(mesh):
    placed = (
        P(("dp", "context", "tensor"), None),
        P(("dp", "context"), "tensor"),
        P(("dp", "context"), "tensor"),
        P(("dp", "context"), None),
        P(("dp", "context"), None),
        P("tensor", ("dp", "context")),
        P("dp", None),
        P(("dp", "context"), "tensor"),
        P("tensor", ("dp", "context")),
        P(),
        P(),
    )
    return jax.shard_map(
        on_device,
        mesh=mesh,
        in_specs=placed,
        out_specs=(P(("dp", "context", "tensor"), None), P(("dp", "context"), "tensor")),
        check_vma=False,
    )
```

```python
import functools
import math

import jax
import jax.numpy as jnp
from jax import lax
from jax.experimental import pallas as pl
from jax.experimental.pallas import tpu as pltpu
from jax.sharding import PartitionSpec as P

MESH = pl.DeviceIdType.MESH
BF = jnp.bfloat16
F32 = jnp.float32
NX, NY, NZ = 4, 4, 8
SPAN = 256
HD = 128
N_REMOTE = 256
N_LOCAL = 16
WINDOW = 8
W_ROWS = 64
Q_ROWS = ((0, 64), (64, 96), (160, 96))
ORDER = (
    "swvrqwgvsrvqswvsrqqsgrggwgggVvqVsggbvVwR",
    "hhhqbVshhrswRVhhbahhcdbwqrcRaVbtdtRcttas",
    "tRqdaRtdcdbsacdtabpcdypppy",
)


def wrap(i, n):
    return lax.rem(i + n, n)


class Links:
    def __init__(self, send, recv):
        self.send, self.recv, self.started = send, recv, []

    def copy(self, src, dst, dev):
        n = len(self.started)
        c = pltpu.make_async_remote_copy(
            src_ref=src,
            dst_ref=dst,
            send_sem=self.send.at[n],
            recv_sem=self.recv.at[n],
            device_id=dev,
            device_id_type=MESH,
        )
        c.start()
        self.started.append(c)
        return c


def ring_gather(links, n, i, slab, half, up, down, arrived=None):
    k = n // 2
    cp = links.copy(slab(i), slab(i), up)
    cm = links.copy(slab(i), slab(i), down)
    if arrived is not None:
        arrived(slab(i))
    for s in range(1, k):
        yield
        before, after = slab(wrap(i - s, n)), slab(wrap(i + s, n))
        cp.wait_recv()
        piece = before if s < k - 1 or half is None else before.at[0:half]
        cp = links.copy(piece, piece, up)
        if arrived is not None:
            arrived(before)
        cm.wait_recv()
        if s < k - 1:
            cm = links.copy(after, after, down)
        elif half is not None:
            piece = after.at[half : 2 * half]
            cm = links.copy(piece, piece, down)
        else:
            cm = None
        if arrived is not None:
            arrived(after)
    yield
    cp.wait_recv()
    if cm is not None:
        cm.wait_recv()
    if arrived is not None:
        arrived(slab(wrap(i + k, n)))


def pipelined_gather(links, z, x, slab, half, z_devs, x_devs):
    zk = NZ // 2
    sent = []

    def along_x(zs):
        ups, downs = [], []
        for zi in zs:
            piece = slab(x, zi)
            ups.append(links.copy(piece, piece, x_devs[0]))
            downs.append(links.copy(piece, piece, x_devs[1]))
        sent.append((zs, ups, downs))

    def first():
        own = slab(x, z)
        cp, cm = links.copy(own, own, z_devs[0]), links.copy(own, own, z_devs[1])
        along_x((z,))
        for s in range(1, zk):
            yield
            before, after = wrap(z - s, NZ), wrap(z + s, NZ)
            cp.wait_recv()
            cm.wait_recv()
            up, down = slab(x, before), slab(x, after)
            if s == zk - 1:
                up, down = up.at[0:half], down.at[half : 2 * half]
            cp, cm = links.copy(up, up, z_devs[0]), links.copy(down, down, z_devs[1])
            along_x((before, after))
        yield
        cp.wait_recv()
        cm.wait_recv()
        along_x((wrap(z + zk, NZ),))

    def second():
        before, after = wrap(x - 1, NX), wrap(x + 1, NX)
        halves = []
        for k in range(zk + 1):
            yield
            zs, ups, downs = sent[k]
            for zi, up, down in zip(zs, ups, downs):
                up.wait_recv()
                down.wait_recv()
                got = slab(before, zi)
                piece = got.at[0:half]
                halves.append(links.copy(piece, piece, x_devs[0]))
                got = slab(after, zi)
                piece = got.at[half : 2 * half]
                halves.append(links.copy(piece, piece, x_devs[1]))
        yield
        for c in halves:
            c.wait_recv()

    return first, second


def spread(links, piece, devs, source=None):
    source = piece if source is None else source
    copies = [links.copy(source, piece, d) for d in devs]
    yield
    for c in copies:
        c.wait_recv()


def ring_reduce(links, n, i, slab, buf, half, up, down):
    k = n // 2
    far = wrap(i + k, n)
    cp = links.copy(slab(far).at[0:half], buf.at[0, 0, 0:half], up)
    cm = links.copy(slab(far).at[half : 2 * half], buf.at[1, 0, half : 2 * half], down)
    yield

    def add(dst, part):
        dst[...] = (dst[...].astype(F32) + part[...].astype(F32)).astype(BF)

    for step in range(1, k):
        s = k - step
        dst = slab(wrap(i + s, n))
        cp.wait_recv()
        if step == 1:
            add(dst.at[0:half], buf.at[0, 0, 0:half])
        else:
            add(dst, buf.at[0, step - 1])
        cp = links.copy(dst, buf.at[0, step], up)
        dst = slab(wrap(i - s, n))
        cm.wait_recv()
        if step == 1:
            add(dst.at[half : 2 * half], buf.at[1, 0, half : 2 * half])
        else:
            add(dst, buf.at[1, step - 1])
        cm = links.copy(dst, buf.at[1, step], down)
        yield
    cp.wait_recv()
    cm.wait_recv()
    dst = slab(i)
    dst[...] = (
        dst[...].astype(F32) + buf[0, k - 1].astype(F32) + buf[1, k - 1].astype(F32)
    ).astype(BF)


def spread_reduce(links, n, i, slab, buf, devs):
    copies = [
        links.copy(slab(wrap(i + step, n)), buf.at[j], d)
        for j, (step, d) in enumerate(zip((1, n - 1, 2), devs))
    ]
    yield
    for c in copies:
        c.wait_recv()
    dst = slab(i)
    total = dst[...].astype(F32)
    for j in range(3):
        total += buf[j].astype(F32)
    dst[...] = total.astype(BF)


def contract(a, b, da, db):
    return lax.dot_general(a, b, (((da,), (db,)), ((), ())), preferred_element_type=F32)


def kernel(
    grad_out, queries_in, attended_in, keys_in, values_in, log_sums_in, seg_in,
    w_out, w_query, w_key, w_value,
    gin_out, dwo,
    queries, attended, keys, values, log_sums, seg, gin, tg, wv, qv, kvw, pb, raz, rax, rbx, rbz, ry,
    halo, ag, att_t, acc, qkv, kvg, kvback, kvland, ab, send, recv, loc,
):
    x = lax.axis_index("dp")
    r = lax.axis_index("context")
    t = lax.axis_index("tensor")
    yl, z = lax.div(r, NZ), lax.rem(r, NZ)
    yh, core = lax.div(t, 2), lax.rem(t, 2)
    y = 2 * yh + yl
    other = 1 - core
    partner = 2 * (1 - yh) + core

    def dev(x, y, z, core):
        return {
            "dp": x,
            "context": lax.rem(y, 2) * NZ + z,
            "tensor": lax.div(y, 2) * 2 + core,
        }

    xp, xm = dev(wrap(x + 1, NX), y, z, core), dev(wrap(x - 1, NX), y, z, core)
    yp, ym = dev(x, wrap(y + 1, NY), z, core), dev(x, wrap(y - 1, NY), z, core)
    zp, zm = dev(x, y, wrap(z + 1, NZ), core), dev(x, y, wrap(z - 1, NZ), core)
    pair = dev(x, 2 * yh + 1 - yl, z, core)
    sib = dev(x, y, z, other)
    far = dev(x, wrap(y + 2, NY), z, core)
    far_x = dev(wrap(x + 2, NX), y, z, core)
    far_sib = dev(x, wrap(y + 2, NY), z, other)
    n_ctx = 2 * NZ
    rp = {"dp": x, "context": wrap(r + 1, n_ctx), "tensor": t}
    rm = {"dp": x, "context": wrap(r - 1, n_ctx), "tensor": t}
    links = Links(send, recv)

    local = [
        pltpu.make_async_copy(w_out, wv.at[x, yl, z], loc.at[0]),
        pltpu.make_async_copy(w_query, qv.at[core, x, y, z], loc.at[1]),
        pltpu.make_async_copy(grad_out, tg.at[t], loc.at[2]),
        pltpu.make_async_copy(w_key, kvw.at[0:HD], loc.at[3]),
        pltpu.make_async_copy(w_value, kvw.at[HD : 2 * HD], loc.at[4]),
        pltpu.make_async_copy(attended_in, attended, loc.at[5]),
        pltpu.make_async_copy(queries_in, queries, loc.at[6]),
        pltpu.make_async_copy(keys_in, keys, loc.at[7]),
        pltpu.make_async_copy(values_in, values, loc.at[8]),
        pltpu.make_async_copy(log_sums_in, log_sums, loc.at[9]),
        pltpu.make_async_copy(seg_in, seg, loc.at[10]),
    ]
    partners = (xp, xm, yp, ym, zp, zm, rp, rm, sib, far, far_sib, far_x)
    barrier = pltpu.get_barrier_semaphore()
    for d in partners:
        pl.semaphore_signal(barrier, inc=1, device_id=d, device_id_type=MESH)
    for c in local:
        c.start()
    pl.semaphore_wait(barrier, len(partners))

    chunk = NZ * HD
    n_chunks = 2 * NX
    ready = set()
    far_copies, own_copy, sib_copies, halo_copies = [], [], [], []

    def cols(j):
        return pl.ds(((j % NX) * 2 + j // NX) * chunk, chunk)

    def send_far():
        j = len(far_copies)
        if j < n_chunks:
            far_copies.append(links.copy(grad_out.at[:, cols(j)], tg.at[t, :, cols(j)], far))

    def dw_chunk(j):
        if j == 0:
            local[2].wait()
            own_copy[0].wait_recv()
        sib_copies[j].wait_recv()
        xi, yi = j % NX, j // NX

        def step(q, carry):
            at = pl.ds(pl.multiple_of((xi * 2 + yi) * chunk + q * 4 * HD, 4 * HD), 4 * HD)
            lhs = tg[:, :, at].reshape(2 * SPAN, 4 * HD)
            part = jnp.dot(att_t[...], lhs, preferred_element_type=F32).astype(BF)
            for u in range(4):
                pb[xi, yi, 4 * q + u] = part[:, u * HD : (u + 1) * HD]
            return carry

        lax.fori_loop(0, 2, step, 0)

    def grads_stream(first):
        yield
        if first == 0:
            for _ in range(WINDOW):
                send_far()
            own_copy.append(links.copy(grad_out, tg.at[t], sib))
        for j in range(first, first + NX):
            yield
            far_copies[j].wait_recv()
            send_far()
            got = tg.at[partner, :, cols(j)]
            sib_copies.append(links.copy(got, got, sib))
            if j > first:
                yield
                dw_chunk(j - 1)
        yield
        dw_chunk(first + NX - 1)

    def w_out_stream(part):
        hs = pl.ds(0, W_ROWS) if part == 0 else pl.ds(W_ROWS, HD - W_ROWS)
        yield
        c = links.copy(w_out.at[hs], wv.at[x, yl, z, hs], pair)
        yield
        if 0 not in ready:
            local[0].wait()
            ready.add(0)
        c.wait_recv()
        if part == 0:
            yield from spread(links, wv.at[x, :, z, hs], (xp, xm, far_x))
            yield from ring_gather(links, NZ, z, lambda i: wv.at[:, :, i, hs], 2, zp, zm)
        else:
            yield from w_first()

    w_rest = pl.ds(W_ROWS, HD - W_ROWS)
    w_first, w_second = pipelined_gather(
        links, z, x, lambda i, j: wv.at[i, :, j, w_rest], 1, (zp, zm), (xp, xm)
    )
    q_waits = []

    def w_query_stream(part):
        lo_row, n_rows = Q_ROWS[part]
        hs = pl.ds(lo_row, n_rows)

        def hand_over(piece):
            q_waits.append(links.copy(piece, piece, sib))

        yield
        if part == 2:
            if 1 not in ready:
                local[1].wait()
                ready.add(1)
            yield from ring_gather(links, NZ, z, lambda i: qv.at[core, x, y, i, hs], None, zp, zm)
            yield from ring_gather(links, NX, x, lambda i: qv.at[core, i, y, :, hs], 4, xp, xm)
            yield
            yield from ring_gather(
                links, NY, y, lambda i: qv.at[core, :, i, :, hs], 2, yp, ym, hand_over
            )
            return
        yield from spread(links, qv.at[core, x, y, z, hs], (yp, ym, far), w_query.at[hs])
        if 1 not in ready:
            local[1].wait()
            ready.add(1)
        if part == 0:
            yield from spread(links, qv.at[core, x, :, z, hs], (xp, xm, far_x))
            yield
            yield from ring_gather(
                links, NZ, z, lambda i: qv.at[core, :, :, i, hs], 2, zp, zm, hand_over
            )
        else:
            yield from q_first()

    q_rest = pl.ds(Q_ROWS[1][0], Q_ROWS[1][1])
    q_first, q_second = pipelined_gather(
        links, z, x, lambda i, j: qv.at[core, i, :, j, q_rest], 2, (zp, zm), (xp, xm)
    )

    def q_tail():
        yield from q_second()
        for i in range(NX):
            piece = qv.at[core, i, :, :, q_rest]
            q_waits.append(links.copy(piece, piece, sib))

    lo, hi = pl.ds(0, HD), pl.ds(HD, HD)

    def reduce_a(yi):
        yield
        yield from ring_reduce(
            links, NZ, z, lambda i: pb.at[:, yi, i, lo], raz.at[yi], 2, zp, zm
        )
        yield from spread_reduce(
            links, NX, x, lambda i: pb.at[i, yi, z, lo], rax.at[yi], (xp, xm, far_x)
        )

    def reduce_b(yi):
        yield
        yield from ring_reduce(
            links, NX, x, lambda i: pb.at[i, yi, :, hi], rbx.at[yi], 4, xp, xm
        )
        yield from ring_reduce(
            links, NZ, z, lambda i: pb.at[x, yi, i, hi], rbz.at[yi], 64, zp, zm
        )

    def pair_sum():
        yield
        c = links.copy(pb.at[x, 1 - yl, z], ry, pair)
        yield
        c.wait_recv()
        dwo[...] = (pb[x, yl, z].astype(F32) + ry[...].astype(F32)).T

    def ag_steps(first):
        def step(j, carry):
            at = pl.ds(pl.multiple_of(j * 4 * HD, 4 * HD), 4 * HD)
            lhs = tg[:, :, at].reshape(2 * SPAN, 4 * HD)
            xi, rest = lax.div(j, 4), lax.rem(j, 4)
            yi, zi = lax.div(rest, 2), lax.rem(rest, 2) * 4
            rhs = wv[xi, yi, pl.ds(zi, 4)].reshape(4 * HD, 2 * HD)
            acc[...] += jnp.dot(lhs, rhs, preferred_element_type=F32)
            return carry

        lax.fori_loop(first, first + 4, step, 0)

    last = r == n_ctx - 1
    inv_root = 1.0 / math.sqrt(HD)
    row_at = lax.broadcasted_iota(jnp.int32, (SPAN, SPAN), 0)
    col_at = lax.broadcasted_iota(jnp.int32, (SPAN, SPAN), 1)
    eye = row_at == col_at
    q_at = lax.broadcasted_iota(jnp.int32, (SPAN, 2 * SPAN), 0)
    k_at = lax.broadcasted_iota(jnp.int32, (SPAN, 2 * SPAN), 1) - SPAN

    def column(row, zero):
        return jnp.sum(jnp.where(eye, row, zero), axis=1, keepdims=True)

    def seg_of(span):
        return seg[:, pl.ds(pl.multiple_of(span * SPAN, SPAN), SPAN)]

    def unit(b, h):
        rows_b, cols_h = pl.ds(b * SPAN, SPAN), pl.ds(h * HD, HD)
        span = r if b == 0 else 2 * n_ctx - 1 - r
        seg_q = seg_of(span)
        seg_k = jnp.concatenate([seg_of(jnp.maximum(span - 1, 0)), seg_q], axis=1)
        allowed = (
            (k_at <= q_at)
            & (k_at + span * SPAN >= 0)
            & (seg_k == column(seg_q, 0))
        )
        prev_k, prev_v = halo[b, 0], halo[b, 1]
        if b == 1:
            prev_k = jnp.where(last, keys[0:SPAN], prev_k)
            prev_v = jnp.where(last, values[0:SPAN], prev_v)
        k_cat = jnp.concatenate([prev_k, keys[rows_b]], axis=0)
        v_cat = jnp.concatenate([prev_v, values[rows_b]], axis=0)
        qb, db = queries[rows_b, cols_h], ag[rows_b, cols_h]
        delta = jnp.sum(
            db.astype(F32) * attended[rows_b, cols_h].astype(F32), axis=1, keepdims=True
        )
        lse = column(log_sums[h : h + 1, rows_b], 0.0)
        scores = contract(qb, k_cat, 1, 1) * inv_root
        prob = jnp.where(allowed, jnp.exp(scores - lse), 0.0)
        dprob = contract(db, v_cat, 1, 1)
        dscore = (prob * (dprob - delta)).astype(BF)
        dq = jnp.dot(dscore, k_cat, preferred_element_type=F32) * inv_root
        qkv[rows_b, cols_h] = dq.astype(BF)
        kg = contract(dscore, qb, 0, 0) * inv_root
        vg = contract(prob.astype(BF), db, 0, 0)
        if h == 0:
            kvg[b, :, 0:HD] = kg
            kvg[b, :, HD : 2 * HD] = vg
        else:
            kvg[b, :, 0:HD] += kg
            kvg[b, :, HD : 2 * HD] += vg

    def rows_of(d):
        return pl.ds(pl.multiple_of(d * HD, HD), HD)

    def attention_stream():
        for part in range(4):
            yield
            if part == 0:
                acc[...] = jnp.zeros_like(acc)
            ag_steps(4 * part)
        yield
        ag[...] = acc[...].astype(BF)
        for c in local[6:]:
            c.wait()
        for c in halo_copies:
            c.wait_recv()
        for b in range(2):
            for h in range(2):
                unit(b, h)
        kvback[0] = kvg[0, 0:SPAN].astype(BF)
        kvback[1] = jnp.where(last, 0.0, kvg[1, 0:SPAN]).astype(BF)
        to_left = links.copy(kvback.at[0], kvland.at[0], rm)
        to_right = links.copy(kvback.at[1], kvland.at[1], rp)
        yield
        to_left.wait_recv()
        to_right.wait_recv()
        low = (
            kvg[0, SPAN : 2 * SPAN]
            + jnp.where(last, kvg[1, 0:SPAN], 0.0)
            + kvland[0].astype(F32)
        )
        high = kvg[1, SPAN : 2 * SPAN] + kvland[1].astype(F32)
        qkv[0:SPAN, 2 * HD : 4 * HD] = low.astype(BF)
        qkv[SPAN : 2 * SPAN, 2 * HD : 4 * HD] = high.astype(BF)
        swaps = [
            links.copy(qkv.at[rows_of(partner)], ab.at[t], far),
            links.copy(qkv.at[rows_of(2 * (1 - yh) + other)], ab.at[t], far_sib),
            links.copy(qkv.at[rows_of(2 * yh + other)], ab.at[t], sib),
        ]
        ab[t] = qkv[rows_of(t)]
        yield
        for c in swaps:
            c.wait_recv()

    out_copies = []

    def out_stream():
        yield
        local[3].wait()
        local[4].wait()
        for c in q_waits:
            c.wait_recv()
        kv_sum = jnp.sum(ab[:, :, 2 * HD : 4 * HD].astype(F32), axis=0).astype(BF)

        def step(j, carry):
            xi, yi = lax.div(j, 2), lax.rem(j, 2)
            for q in range(4):
                at = pl.ds(pl.multiple_of(j * chunk + q * 2 * HD, 2 * HD), 2 * HD)
                total = jnp.dot(kv_sum, kvw[:, at], preferred_element_type=F32)
                for g in range(4):
                    heads = qv.at[g % 2, xi, 2 * (g // 2) + yi]
                    rhs = jnp.concatenate([heads[2 * q], heads[2 * q + 1]], axis=1)
                    total += jnp.dot(ab[g, :, 0 : 2 * HD], rhs, preferred_element_type=F32)
                gin[:, at] = total.astype(BF)
            return carry

        for part in range(4):
            lax.fori_loop(2 * part, 2 * part + 2, step, 0)
            at = pl.ds(2 * part * chunk, 2 * chunk)
            out_copies.append(pltpu.make_async_copy(gin.at[:, at], gin_out.at[:, at], loc.at[11 + part]))
            out_copies[-1].start()
            if part < 3:
                yield

    live = {
        "w": w_out_stream(0),
        "v": w_out_stream(1),
        "g": grads_stream(0),
        "h": grads_stream(NX),
        "q": w_query_stream(0),
        "r": w_query_stream(1),
        "s": w_query_stream(2),
        "a": reduce_a(0),
        "b": reduce_b(0),
        "c": reduce_a(1),
        "d": reduce_b(1),
        "y": pair_sum(),
        "t": attention_stream(),
        "p": out_stream(),
        "V": w_second(),
        "R": q_tail(),
    }
    for stream in live.values():
        next(stream)
    for n, name in enumerate("".join(ORDER)):
        next(live[name], 0)
        if n == 5:
            halo_copies.extend([
                links.copy(keys_in.at[0:SPAN], halo.at[0, 0], rp),
                links.copy(values_in.at[0:SPAN], halo.at[0, 1], rp),
                links.copy(keys_in.at[SPAN : 2 * SPAN], halo.at[1, 0], rm),
                links.copy(values_in.at[SPAN : 2 * SPAN], halo.at[1, 1], rm),
            ])
            local[5].wait()
            att_t[...] = attended[...].astype(F32).T.astype(BF)
    for stream in live.values():
        assert next(stream, 0) == 0
    for c in links.started:
        c.wait_send()
    for c in out_copies:
        c.wait()


N_OUT = 4


def hand_out(gin, dwo, gin_out, dwo_out, gin_here, dwo_here, sems):
    rows = gin.shape[0] // N_OUT
    parts = [(gin.at[at], gin_here.at[at], gin_out.at[at]) for at in (pl.ds(k * rows, rows) for k in range(N_OUT))]
    parts.append((dwo, dwo_here, dwo_out))
    loads = [pltpu.make_async_copy(a, b, sems.at[0, k]) for k, (a, b, _) in enumerate(parts)]
    stores = [pltpu.make_async_copy(b, c, sems.at[1, k]) for k, (_, b, c) in enumerate(parts)]
    for c in loads:
        c.start()
    for load, store in zip(loads, stores):
        load.wait()
        store.start()
    for c in stores:
        c.wait()


def on_device(
    grad_out, queries, attended, keys, values, log_sums, segment_ids, w_out, w_query, w_key, w_value
):
    vmem = pl.BlockSpec(memory_space=pltpu.VMEM)
    hbm = pl.BlockSpec(memory_space=pl.ANY)
    own, model = grad_out.shape
    blocks = (NX, 2, NZ)
    results = pl.pallas_call(
        kernel,
        out_shape=(
            jax.ShapeDtypeStruct((own, model), BF),
            jax.ShapeDtypeStruct((HD, 2 * HD), F32),
        ),
        in_specs=[hbm] * 11,
        out_specs=(hbm, vmem),
        scratch_shapes=[
            pltpu.VMEM(queries.shape, BF),
            pltpu.VMEM(attended.shape, BF),
            pltpu.VMEM(keys.shape, BF),
            pltpu.VMEM(values.shape, BF),
            pltpu.VMEM(log_sums.shape, F32),
            pltpu.VMEM(segment_ids.shape, jnp.int32),
            pltpu.VMEM((own, model), BF),
            pltpu.VMEM((4, own, model), BF),
            pltpu.VMEM(blocks + (HD, 2 * HD), BF),
            pltpu.VMEM((2, NX, NY, NZ, 2 * HD, HD), BF),
            pltpu.VMEM((2 * HD, model), BF),
            pltpu.VMEM(blocks + (2 * HD, HD), BF),
            pltpu.VMEM((2, 2, 4, NX, HD, HD), BF),
            pltpu.VMEM((2, 3, HD, HD), BF),
            pltpu.VMEM((2, 2, 2, NZ, HD, HD), BF),
            pltpu.VMEM((2, 2, 4, HD, HD), BF),
            pltpu.VMEM((2 * HD, HD), BF),
            pltpu.VMEM((2, 2, SPAN, HD), BF),
            pltpu.VMEM((2 * SPAN, 2 * HD), BF),
            pltpu.VMEM((2 * HD, 2 * SPAN), BF),
            pltpu.VMEM((2 * SPAN, 2 * HD), F32),
            pltpu.VMEM((2 * SPAN, 4 * HD), BF),
            pltpu.VMEM((2, 2 * SPAN, 2 * HD), F32),
            pltpu.VMEM((2, SPAN, 2 * HD), BF),
            pltpu.VMEM((2, SPAN, 2 * HD), BF),
            pltpu.VMEM((4, HD, 4 * HD), BF),
            pltpu.SemaphoreType.DMA((N_REMOTE,)),
            pltpu.SemaphoreType.DMA((N_REMOTE,)),
            pltpu.SemaphoreType.DMA((N_LOCAL,)),
        ],
        compiler_params=pltpu.CompilerParams(
            collective_id=0, has_side_effects=True, vmem_limit_bytes=60 * 2**20
        ),
    )(
        grad_out, queries, attended, keys, values, log_sums, segment_ids, w_out, w_query, w_key, w_value
    )
    return pl.pallas_call(
        hand_out,
        out_shape=(
            jax.ShapeDtypeStruct((own, model), BF),
            jax.ShapeDtypeStruct((HD, 2 * HD), F32),
        ),
        in_specs=[hbm, hbm],
        out_specs=(hbm, hbm),
        scratch_shapes=[
            pltpu.VMEM((own, model), BF),
            pltpu.VMEM((HD, 2 * HD), F32),
            pltpu.SemaphoreType.DMA((2, N_OUT + 1)),
        ],
        compiler_params=pltpu.CompilerParams(vmem_limit_bytes=60 * 2**20),
    )(*results)


def solution(mesh):
    placed = (
        P(("dp", "context", "tensor"), None),
        P(("dp", "context"), "tensor"),
        P(("dp", "context"), "tensor"),
        P(("dp", "context"), None),
        P(("dp", "context"), None),
        P("tensor", ("dp", "context")),
        P("dp", None),
        P(("dp", "context"), "tensor"),
        P("tensor", ("dp", "context")),
        P(),
        P(),
    )
    return jax.shard_map(
        on_device,
        mesh=mesh,
        in_specs=placed,
        out_specs=(P(("dp", "context", "tensor"), None), P(("dp", "context"), "tensor")),
        check_vma=False,
    )
```
